32 devices in a mesh: grp: 2 (over y), tile: 4 (over z), sub: 4 (over x, core).
Axes of the slice: x: 2, y: 2, z: 4, core: 2. Of those that a mesh axis runs over, the one named last changes fastest.
Arguments:
- features: bfloat16 [24, 32, 1024], P(('grp', 'tile'), 'sub'), parts along dimension 0, may hold values from -6 to 6
- out_grad: bfloat16 [24, 32, 1024], P(('grp', 'tile'), 'sub'), parts along dimension 0, may hold values from -6 to 6
- filters: bfloat16 [5, 32, 32], replicated, may hold values from -0.5 to 0.5
- tile_map: int32 [12], replicated, may hold values from 0 to 11, as said below
Outputs:
- in_grad: bfloat16 [24, 32, 1024], P(('grp', 'tile'), 'sub'), parts along dimension 0
- weight_grad: float32 [10, 32, 32], P('grp', 'sub'), parts along dimension 0
The draws below stay inside these ranges and needn't reach their ends.
There are 2 independent parts, one for each index of `grp`. The reference program is written for one: setup_inputs(seed, part) draws one part's arguments, and reference() takes and returns one part's arrays. A program takes and returns all parts, laid end to end along the dimension named above; an argument that names none is the same for every part. Nothing has to cross between parts.
Inputs may be any that keep to these rules, and one draw needn't show every extreme that they name: tile_map[s] is the nested index of the tile held in slot s; slots 3 * j to 3 * j + 2 lie on index j of tile and hold the nested indices 3 * j to 3 * j + 2 in some order.
All inputs are finite; a program needn't handle non-finite values.
Results may differ from the reference program's by a relative error of at most 0.00045.
Values may be sent and summed in bfloat16 or wider, within the bound.
A program may use at most 64 MiB of HBM per device.

```python
import math
import jax
import jax.numpy as jnp
from jax import lax

C = 32
K = 5
TPD = 3
TS = 32
Q = 1
TILES = 12
PIXELS = 12288


def draw_tile_map(key, part):
    blocks = jnp.arange(TILES, dtype=jnp.int32).reshape(TILES // TPD, TPD)
    shuffled = jax.random.permutation(key, blocks, axis=1, independent=True)
    return shuffled.reshape(TILES).astype(jnp.int32)


def shard_levels(stream_key, shape, pieces, smallest, largest):
    def one(dim, blocks):
        draws = jax.random.uniform(jax.random.fold_in(jax.random.fold_in(stream_key, 6), dim), (blocks,), jnp.float32, smallest / len(pieces), largest / len(pieces))
        return jnp.repeat(jnp.exp(draws), shape[dim] // blocks).reshape((-1,) + (1,) * (len(shape) - dim - 1))

    factor_of = one(*pieces[0])
    for cut in pieces[1:]:
        factor_of = factor_of * one(*cut)
    return factor_of


def noise(own_key, shape, spread, limit, cuts=(), kind=jnp.bfloat16):
    result = jax.random.normal(own_key, shape, jnp.float32) * spread
    if len(cuts) > 0:
        result = shard_levels(own_key, shape, cuts, -0.22, 0.18) * result
    return jnp.clip(result, min=-limit, max=limit).astype(kind)


def setup_inputs(seed: int = 0, part: int = 0) -> dict:
    streams_of = jax.random.split(jax.random.key(seed), 5)
    own_keys = jax.random.split(jax.random.fold_in(streams_of[4], part), 5)
    features = noise(own_keys[0], (TILES, C, TS * TS), 1.0, 6.0, ((0, 4), (1, 4)))
    out_grad = noise(own_keys[1], (TILES, C, TS * TS), 1.0, 6.0, ((0, 4), (1, 4)))
    filters = noise(streams_of[2], (K, C, C), (K * C) ** -0.5, 0.5)
    tile_map = draw_tile_map(jax.random.fold_in(streams_of[4], 71), part)
    return dict(features=features, out_grad=out_grad, filters=filters, tile_map=tile_map)


def tile_coords(nested_code, bit_count):
    coord_x = nested_code * 0
    coord_y = nested_code * 0
    for bit_level in range(bit_count):
        coord_x = coord_x + nested_code // 4 ** bit_level % 2 * 2 ** bit_level
        coord_y = coord_y + nested_code // (2 * 4 ** bit_level) % 2 * 2 ** bit_level
    return (coord_x, coord_y)

def nested_index(coord_x, coord_y, bit_count):
    nested_code = coord_x * 0
    for bit_level in range(bit_count):
        nested_code = nested_code + coord_x // 2 ** bit_level % 2 * 4 ** bit_level
        nested_code = nested_code + coord_y // 2 ** bit_level % 2 * (2 * 4 ** bit_level)
    return nested_code

def pick(condition, when_true, when_false):
    return when_false + (when_true - when_false) * condition

def neighbour_codes(tile_ids, per_face, side_count):
    bit_count = side_count.bit_length() - 1
    face_id = tile_ids // per_face
    coord_x, coord_y = tile_coords(tile_ids % per_face, bit_count)
    column = face_id % 4
    is_north = face_id < 4
    is_south = face_id >= 8
    last_tile = side_count - 1

    def by_cycle(north_value, equator_value, south_value):
        return pick(is_north, north_value, pick(is_south, south_value, equator_value))
    side_rules = [(coord_x > 0, (face_id, coord_x - 1, coord_y, 1), (by_cycle(4 + column, 8 + (column + 3) % 4, 8 + (column + 3) % 4), by_cycle(last_tile, last_tile, coord_y), by_cycle(coord_y, coord_y, 0), by_cycle(1, 1, 2))), (coord_x < last_tile, (face_id, coord_x + 1, coord_y, 0), (by_cycle((column + 1) % 4, column, 4 + (column + 1) % 4), by_cycle(coord_y, 0, 0), by_cycle(last_tile, coord_y, coord_y), by_cycle(3, 0, 0))), (coord_y > 0, (face_id, coord_x, coord_y - 1, 3), (by_cycle(4 + (column + 1) % 4, 8 + column, 8 + (column + 1) % 4), by_cycle(coord_x, coord_x, 0), by_cycle(last_tile, last_tile, coord_x), by_cycle(3, 3, 0))), (coord_y < last_tile, (face_id, coord_x, coord_y + 1, 2), (by_cycle((column + 3) % 4, (column + 3) % 4, 4 + column), by_cycle(last_tile, coord_x, coord_x), by_cycle(coord_x, 0, 0), by_cycle(1, 2, 2)))]
    target_list = []
    edge_list = []
    for inside, within, across in side_rules:
        chosen = [pick(inside, near_value, far_value) for near_value, far_value in zip(within, across)]
        target_list.append(chosen[0] * per_face + nested_index(chosen[1], chosen[2], bit_count))
        edge_list.append(chosen[3] + tile_ids * 0)
    return (target_list, edge_list)

def neighbour_table(tile_map, per_face, side_count):
    target_list, edge_list = neighbour_codes(tile_map, per_face, side_count)
    targets = jnp.stack(target_list, axis=1).astype(jnp.int32)
    edges = jnp.stack(edge_list, axis=1).astype(jnp.int32)
    slot_of = jnp.argsort(tile_map).astype(jnp.int32)
    return (slot_of[targets].astype(jnp.int32), edges)

def edge_lines(values, tile_side):
    return jnp.stack([values[..., :tile_side], values[..., -tile_side:], values[..., ::tile_side], values[..., tile_side - 1::tile_side]], axis=1)

def stencil(values, ghosts, tile_side):
    position = jnp.arange(values.shape[-1]) % tile_side
    zero_line = jnp.zeros_like(values[..., :1])
    upper_side = jnp.concatenate([ghosts[:, 0], values[..., :-tile_side]], axis=-1)
    lower_side = jnp.concatenate([values[..., tile_side:], ghosts[:, 1]], axis=-1)
    left_side = jnp.where(position == 0, jnp.repeat(ghosts[:, 2], tile_side, axis=-1), jnp.concatenate([zero_line, values[..., :-1]], axis=-1))
    right_side = jnp.where(position == tile_side - 1, jnp.repeat(ghosts[:, 3], tile_side, axis=-1), jnp.concatenate([values[..., 1:], zero_line], axis=-1))
    return -0.25 * (upper_side + lower_side + left_side + right_side)

def reference(features, out_grad, filters, tile_map):
    slot_table, edge_table = neighbour_table(tile_map, TILES // 12, Q)
    highest = lax.Precision.HIGHEST

    def laplace(values):
        return stencil(values, edge_lines(values, TS)[slot_table, edge_table], TS)
    inputs = features.astype(jnp.float32)
    cotangent = out_grad.astype(jnp.float32)
    weights = filters.astype(jnp.float32)
    previous, current = (inputs, laplace(inputs))
    filter_terms = [jnp.einsum('sip,sop->io', inputs, cotangent, precision=highest), jnp.einsum('sip,sop->io', current, cotangent, precision=highest)]
    for degree in range(2, K):
        previous, current = (current, 2.0 * laplace(current) - previous)
        filter_terms.append(jnp.einsum('sip,sop->io', current, cotangent, precision=highest))
    weight_grad = jnp.stack(filter_terms) / math.sqrt(PIXELS)

    def mixed(degree):
        return jnp.einsum('sop,io->sip', cotangent, weights[degree], precision=highest)
    next_sum = mixed(K - 1)
    after_next = jnp.zeros_like(next_sum)
    for degree in range(K - 2, 0, -1):
        next_sum, after_next = (mixed(degree) + 2.0 * laplace(next_sum) - after_next, next_sum)
    in_grad = (mixed(0) + laplace(next_sum) - after_next).astype(jnp.bfloat16)
    return (in_grad, weight_grad)
```

```python
import functools
import math

import jax
import jax.numpy as jnp
import numpy as np
from jax import lax
from jax.experimental import pallas as pl
from jax.experimental.pallas import tpu as pltpu
from jax.sharding import PartitionSpec as P

K = 5


def from_behind(value, axis, steps):
    count = lax.axis_size(axis)
    pairs = [(source, (source + steps) % count) for source in range(count)]
    return lax.ppermute(value, axis, pairs)


def tile_coords(nested_code, bit_count):
    coord_x = nested_code * 0
    coord_y = nested_code * 0
    for bit_level in range(bit_count):
        coord_x = coord_x + nested_code // 4**bit_level % 2 * 2**bit_level
        coord_y = coord_y + nested_code // (2 * 4**bit_level) % 2 * 2**bit_level
    return (coord_x, coord_y)


def nested_index(coord_x, coord_y, bit_count):
    nested_code = coord_x * 0
    for bit_level in range(bit_count):
        nested_code = nested_code + coord_x // 2**bit_level % 2 * 4**bit_level
        nested_code = nested_code + coord_y // 2**bit_level % 2 * (2 * 4**bit_level)
    return nested_code


def pick(condition, when_true, when_false):
    return when_false + (when_true - when_false) * condition


def neighbour_codes(tile_ids, per_face, side_count):
    bit_count = side_count.bit_length() - 1
    face_id = tile_ids // per_face
    coord_x, coord_y = tile_coords(tile_ids % per_face, bit_count)
    column = face_id % 4
    is_north = face_id < 4
    is_south = face_id >= 8
    last_tile = side_count - 1

    def by_cycle(north_value, equator_value, south_value):
        return pick(is_north, north_value, pick(is_south, south_value, equator_value))

    side_rules = [
        (
            coord_x > 0,
            (face_id, coord_x - 1, coord_y, 1),
            (
                by_cycle(4 + column, 8 + (column + 3) % 4, 8 + (column + 3) % 4),
                by_cycle(last_tile, last_tile, coord_y),
                by_cycle(coord_y, coord_y, 0),
                by_cycle(1, 1, 2),
            ),
        ),
        (
            coord_x < last_tile,
            (face_id, coord_x + 1, coord_y, 0),
            (
                by_cycle((column + 1) % 4, column, 4 + (column + 1) % 4),
                by_cycle(coord_y, 0, 0),
                by_cycle(last_tile, coord_y, coord_y),
                by_cycle(3, 0, 0),
            ),
        ),
        (
            coord_y > 0,
            (face_id, coord_x, coord_y - 1, 3),
            (
                by_cycle(4 + (column + 1) % 4, 8 + column, 8 + (column + 1) % 4),
                by_cycle(coord_x, coord_x, 0),
                by_cycle(last_tile, last_tile, coord_x),
                by_cycle(3, 3, 0),
            ),
        ),
        (
            coord_y < last_tile,
            (face_id, coord_x, coord_y + 1, 2),
            (
                by_cycle((column + 3) % 4, (column + 3) % 4, 4 + column),
                by_cycle(last_tile, coord_x, coord_x),
                by_cycle(coord_x, 0, 0),
                by_cycle(1, 2, 2),
            ),
        ),
    ]
    target_list = []
    edge_list = []
    for inside, within, across in side_rules:
        chosen = [
            pick(inside, near_value, far_value) for near_value, far_value in zip(within, across)
        ]
        target_list.append(chosen[0] * per_face + nested_index(chosen[1], chosen[2], bit_count))
        edge_list.append(chosen[3] + tile_ids * 0)
    return (target_list, edge_list)


def neighbour_table(tile_map, per_face, side_count):
    target_list, edge_list = neighbour_codes(tile_map, per_face, side_count)
    targets = jnp.stack(target_list, axis=1).astype(jnp.int32)
    edges = jnp.stack(edge_list, axis=1).astype(jnp.int32)
    slot_of = jnp.argsort(tile_map).astype(jnp.int32)
    return (slot_of[targets].astype(jnp.int32), edges)


def peer_offsets(slot_count, device_count, per_face, side_count):
    tile_ids = np.arange(slot_count * device_count, dtype=np.int64)
    target_list, edge_list = neighbour_codes(tile_ids, per_face, side_count)
    targets = np.stack(target_list, axis=1)
    offsets = (tile_ids[:, None] // slot_count - targets // slot_count) % device_count
    distinct = sorted(set((int(value) for value in offsets.ravel())) - {0})
    position = np.zeros(device_count, dtype=np.int32)
    for order, value in enumerate(distinct):
        position[value] = order + 1
    return (distinct, position)


def edge_lines(values, tile_side):
    return jnp.stack(
        [
            values[..., :tile_side],
            values[..., -tile_side:],
            values[..., ::tile_side],
            values[..., tile_side - 1 :: tile_side],
        ],
        axis=1,
    )


def stencil(values, ghosts, tile_side):
    position = jnp.arange(values.shape[-1]) % tile_side
    zero_line = jnp.zeros_like(values[..., :1])
    upper_side = jnp.concatenate([ghosts[:, 0], values[..., :-tile_side]], axis=-1)
    lower_side = jnp.concatenate([values[..., tile_side:], ghosts[:, 1]], axis=-1)
    left_side = jnp.where(
        position == 0,
        jnp.repeat(ghosts[:, 2], tile_side, axis=-1),
        jnp.concatenate([zero_line, values[..., :-1]], axis=-1),
    )
    right_side = jnp.where(
        position == tile_side - 1,
        jnp.repeat(ghosts[:, 3], tile_side, axis=-1),
        jnp.concatenate([values[..., 1:], zero_line], axis=-1),
    )
    return -0.25 * (upper_side + lower_side + left_side + right_side)


def tile_total(filter_part):
    return lax.psum(filter_part, "tile")


def general_path(features, out_grad, filters, tile_map):
    slot_count = features.shape[0]
    group_channels = features.shape[1]
    tile_side = math.isqrt(features.shape[2])
    device_count = lax.axis_size("tile")
    total_tiles = slot_count * device_count
    side_count = math.isqrt(total_tiles // 12)
    scale_factor = 1.0 / math.sqrt(total_tiles * features.shape[2])
    highest = lax.Precision.HIGHEST
    slot_table, edge_table = neighbour_table(tile_map, total_tiles // 12, side_count)
    my_device = lax.axis_index("tile")
    first_slot = my_device * slot_count
    my_slots = lax.dynamic_slice_in_dim(slot_table, first_slot, slot_count, 0)
    my_edges = lax.dynamic_slice_in_dim(edge_table, first_slot, slot_count, 0)
    channel_start = lax.axis_index("sub") * group_channels
    weights = filters.astype(jnp.float32)
    distinct, position = peer_offsets(slot_count, device_count, total_tiles // 12, side_count)
    sender_gap = (my_device - my_slots // slot_count) % device_count
    local_rows = jnp.asarray(position)[sender_gap] * slot_count + my_slots % slot_count

    def laplace(values):
        border = edge_lines(values, tile_side).reshape(slot_count, 4, group_channels * tile_side)
        received = [border]
        for offset_value in distinct:
            received.append(from_behind(border, "tile", offset_value))
        stacked = jnp.concatenate(received, axis=0)
        stacked = stacked.reshape(stacked.shape[0], 4, group_channels, tile_side)
        ghosts = stacked[local_rows, my_edges]
        return stencil(values, ghosts, tile_side)

    whole_grad = lax.all_gather(out_grad, "sub", axis=1, tiled=True)
    cotangent = whole_grad.astype(jnp.float32)
    inputs = features.astype(jnp.float32)
    previous, current = (inputs, laplace(inputs))
    filter_terms = [
        jnp.einsum("sip,sop->io", inputs, cotangent, precision=highest),
        jnp.einsum("sip,sop->io", current, cotangent, precision=highest),
    ]
    for degree in range(2, K):
        previous, current = (current, 2.0 * laplace(current) - previous)
        filter_terms.append(jnp.einsum("sip,sop->io", current, cotangent, precision=highest))
    weight_grad = tile_total(jnp.stack(filter_terms)) * scale_factor
    row_block = lax.dynamic_slice_in_dim(weights, channel_start, group_channels, 1)

    def mixed(degree):
        return jnp.einsum("sop,io->sip", cotangent, row_block[degree], precision=highest)

    next_sum = mixed(K - 1)
    after_next = jnp.zeros_like(next_sum)
    for degree in range(K - 2, 0, -1):
        next_sum, after_next = (mixed(degree) + 2.0 * laplace(next_sum) - after_next, next_sum)
    in_grad = (mixed(0) + laplace(next_sum) - after_next).astype(jnp.bfloat16)
    return (in_grad, weight_grad)


DEPTH = K - 1
GHOST_SIDES = (0, 2, 3, 1)


def face_graph(tile_side):
    tile_ids = np.arange(12, dtype=np.int64)
    target_list, edge_list = neighbour_codes(tile_ids, 1, 1)
    targets = np.stack(target_list, axis=1)
    edges = np.stack(edge_list, axis=1)
    pixels = tile_side * tile_side
    grid = np.arange(pixels).reshape(tile_side, tile_side)
    lines = [grid[0], grid[-1], grid[:, 0], grid[:, -1]]
    ghosts = np.zeros((12, 4, tile_side), dtype=np.int64)
    around = np.zeros((12, 4, tile_side, tile_side), dtype=np.int64)
    for tile in range(12):
        for side in range(4):
            ghosts[tile, side] = targets[tile, side] * pixels + lines[edges[tile, side]]
        whole = tile * pixels + grid
        around[tile, 0] = np.concatenate([ghosts[tile, 0][None], whole[:-1]], 0)
        around[tile, 1] = np.concatenate([whole[1:], ghosts[tile, 1][None]], 0)
        around[tile, 2] = np.concatenate([ghosts[tile, 2][:, None], whole[:, :-1]], 1)
        around[tile, 3] = np.concatenate([whole[:, 1:], ghosts[tile, 3][:, None]], 1)
    around = around.transpose(0, 2, 3, 1).reshape(12 * pixels, 4)
    return targets, edges, ghosts, around


@functools.lru_cache(None)
def ghost_tables(tile_side):
    targets, edges, ghosts, around = face_graph(tile_side)
    pixels = tile_side * tile_side
    grid = np.arange(pixels).reshape(tile_side, tile_side)
    strips = np.stack(
        [
            grid[:DEPTH].ravel(),
            grid[-DEPTH:].ravel(),
            grid[:, :DEPTH].T.ravel(),
            grid[:, -DEPTH:].T.ravel(),
        ]
    )
    table = np.zeros((12, 10), dtype=np.int32)
    by_class = []
    for tile in range(12):
        wanted = np.concatenate([ghosts[tile, side] for side in GHOST_SIDES])
        power = np.zeros((wanted.size, 12 * pixels), dtype=np.int32)
        power[np.arange(wanted.size), wanted] = 1
        powers = [power]
        for _ in range(DEPTH - 1):
            powers.append(sum(powers[-1][:, around[:, side]] for side in range(4)))
        rows = np.concatenate(
            [powers[0], powers[1], powers[2] - 8 * powers[0], powers[3] - 12 * powers[1]]
        )
        support = np.flatnonzero(np.any(rows != 0, axis=0))
        sources = [(int(targets[tile, side]), int(edges[tile, side])) for side in range(4)]
        sources += [(tile, side) for side in range(4)]
        covered = set(int(t) * pixels + int(p) for t, e in sources for p in strips[e])
        left = [int(p) for p in support if int(p) not in covered]
        corner_tiles = {}
        for pixel in left:
            corner_tiles.setdefault(pixel // pixels, []).append(pixel % pixels)
        first = lambda t: int(
            np.flatnonzero(np.any(rows[:, [t * pixels + p for p in corner_tiles[t]]] != 0, axis=1))[0]
        )
        for other in sorted(corner_tiles, key=first):
            choice = [e for e in range(4) if set(corner_tiles[other]) <= set(strips[e].tolist())]
            sources.append((other, choice[0]))
        assert len(sources) <= 10
        while len(sources) < 10:
            sources.append(sources[-1])
        table[tile] = [t * 4 + e for t, e in sources]
        lanes = np.concatenate([t * pixels + strips[e] for t, e in sources])
        seen, keep = set(), np.zeros(lanes.size, dtype=bool)
        for lane, pixel in enumerate(lanes.tolist()):
            keep[lane] = pixel not in seen
            seen.add(pixel)
        assert set(support.tolist()) <= seen
        matrix = (rows[:, lanes] * keep[None]).T
        assert np.abs(matrix).max() <= 127
        if tile % 4 == 0:
            by_class.append(matrix)
        else:
            assert np.array_equal(matrix, by_class[-1])
    spread = np.zeros((4, tile_side, tile_side, tile_side), dtype=np.float32)
    step = np.arange(tile_side)
    spread[0, step, 0, step] = 1
    spread[1, step, step, 0] = 1
    spread[2, step, step, -1] = 1
    spread[3, step, -1, step] = 1
    spread = spread.reshape(4 * tile_side, pixels)
    take = np.zeros((pixels, 2 * DEPTH * tile_side), dtype=np.float32)
    take[np.concatenate([strips[2], strips[3]]), np.arange(2 * DEPTH * tile_side)] = 1
    return np.stack(by_class).astype(np.int8), table.reshape(-1), spread, take


def face_kernel(
    sizes,
    x_ref,
    g_ref,
    f_ref,
    map_ref,
    table_ref,
    ghost_hbm,
    spread_hbm,
    take_hbm,
    in_ref,
    w_ref,
    strips,
    x_all,
    part,
    part_in,
    block,
    block_in,
    ghost_raw,
    ghost,
    spread,
    take,
    load_sem,
    s_send,
    s_recv,
    x_send,
    x_recv,
    p_send,
    p_recv,
    w_send,
    w_recv,
):
    slots, tiles_n, subs, side, scale = sizes
    chans = x_ref.shape[1]
    pixels = side * side
    width = DEPTH * side
    j = lax.axis_index("tile")
    s = lax.axis_index("sub")
    tile_peers = [lax.rem(j + d, tiles_n) for d in range(1, tiles_n)]
    sub_peers = [lax.rem(s + d, subs) for d in range(1, subs)]
    every = [(d, e) for d in range(tiles_n) for e in range(subs) if d + e > 0]

    def device(d, e):
        return {"tile": lax.rem(j + d, tiles_n), "sub": lax.rem(s + e, subs)}

    barrier = pltpu.get_barrier_semaphore()
    for d, e in every:
        pl.semaphore_signal(
            barrier, inc=1, device_id=device(d, e), device_id_type=pl.DeviceIdType.MESH
        )
    loads = [
        pltpu.make_async_copy(take_hbm, take, load_sem.at[0]),
        pltpu.make_async_copy(spread_hbm, spread, load_sem.at[1]),
    ]
    for m in range(slots):
        kind = (slots * j + m) // 4
        loads.append(
            pltpu.make_async_copy(ghost_hbm.at[kind], ghost_raw.at[m], load_sem.at[2 + m])
        )
    for copy in loads:
        copy.start()

    base = slots * j

    def slot_of(m):
        found = 0
        for slot in range(1, slots):
            found = jnp.where(map_ref[base + slot] == base + m, slot, found)
        return found

    slot_list = [slot_of(m) for m in range(slots)]
    own = [g_ref[slot_list[m]].astype(jnp.float32) for m in range(slots)]
    stacked = jnp.concatenate(own, axis=0).astype(jnp.bfloat16)
    loads[0].wait()
    cut = jnp.dot(stacked, take[...], preferred_element_type=jnp.float32)
    for m in range(slots):
        rows = slice(m * chans, (m + 1) * chans)
        row = (base + m) * 4
        strips[row] = own[m][:, :width].astype(jnp.bfloat16)
        strips[row + 1] = own[m][:, pixels - width :].astype(jnp.bfloat16)
        strips[row + 2] = cut[rows, :width].astype(jnp.bfloat16)
        strips[row + 3] = cut[rows, width:].astype(jnp.bfloat16)
    pl.semaphore_wait(barrier, len(every))

    def strip_copy(d, sender, target):
        mine = strips.at[pl.ds(sender * slots * 4, slots * 4)]
        return pltpu.make_async_remote_copy(
            mine,
            mine,
            s_send.at[d],
            s_recv.at[sender],
            device_id={"tile": target},
            device_id_type=pl.DeviceIdType.MESH,
        )

    def x_copy(d, sender, target):
        return pltpu.make_async_remote_copy(
            x_ref,
            x_all.at[sender],
            x_send.at[d],
            x_recv.at[sender],
            device_id={"sub": target},
            device_id_type=pl.DeviceIdType.MESH,
        )

    def part_copy(m, d, sender, target):
        return pltpu.make_async_remote_copy(
            part.at[m, target],
            part_in.at[m, sender],
            p_send.at[m, d],
            p_recv.at[m, sender],
            device_id={"sub": target},
            device_id_type=pl.DeviceIdType.MESH,
        )

    def block_copy(order, d, e, sender):
        return pltpu.make_async_remote_copy(
            block.at[lax.rem(s + e, subs)],
            block_in.at[sender],
            w_send.at[order],
            w_recv.at[sender],
            device_id=device(d, e),
            device_id_type=pl.DeviceIdType.MESH,
        )

    for d, peer in enumerate(tile_peers):
        strip_copy(d, j, peer).start()
    for d, peer in enumerate(sub_peers):
        x_copy(d, s, peer).start()

    total_rows = (2 * K - 1) * chans
    row_k = lax.broadcasted_iota(jnp.int32, (subs * chans, total_rows), 1) // chans
    row_o = lax.broadcasted_iota(jnp.int32, (subs * chans, total_rows), 1) % chans
    from_o = lax.broadcasted_iota(jnp.int32, (subs * chans, total_rows), 0)
    mine_o = from_o == row_o + chans * s
    mixing = jnp.zeros((subs * chans, total_rows), jnp.float32)
    for k in range(K):
        chosen = jnp.where(mine_o & ((row_k + 1) // 2 == k), 1.0, 0.0).astype(jnp.bfloat16)
        mixing = mixing + jnp.dot(f_ref[k], chosen, preferred_element_type=jnp.float32)
    mixing = mixing.astype(jnp.bfloat16)

    for copy in loads[1:]:
        copy.wait()
    chunk = 128

    def widen(step, carry):
        at = pl.ds(pl.multiple_of(step * chunk, chunk), chunk)
        for m in range(slots):
            ghost[m, at, :] = ghost_raw[m, at, :].astype(jnp.float32).astype(jnp.bfloat16)
        return carry

    lax.fori_loop(0, ghost.shape[1] // chunk, widen, 0)

    for d, peer in enumerate(tile_peers):
        strip_copy(d, peer, peer).wait_recv()
    lane = lax.broadcasted_iota(jnp.int32, (chans, pixels), 1)
    y_at = lane % side
    scales = (1.0, -0.25, 0.125, -0.0625)
    grad = jnp.zeros((subs * chans, total_rows), jnp.float32)
    terms = []
    for m in range(slots):
        pieces = [
            strips[table_ref[(base + m) * 10 + r]].astype(jnp.float32) for r in range(10)
        ]
        source = jnp.concatenate(pieces, axis=1).astype(jnp.bfloat16)
        lines = jnp.dot(source, ghost[m], preferred_element_type=jnp.float32)
        lines = jnp.concatenate(
            [lines[:, k * 4 * side : (k + 1) * 4 * side] * scales[k] for k in range(DEPTH)], axis=0
        )
        high = lines.astype(jnp.bfloat16).astype(jnp.float32)
        rest = lines - high
        middle = rest.astype(jnp.bfloat16).astype(jnp.float32)
        split = jnp.concatenate([high, middle, rest - middle], axis=0).astype(jnp.bfloat16)
        outer = jnp.dot(split, spread[...], preferred_element_type=jnp.float32)
        count = DEPTH * chans
        outer = outer[:count] + outer[count : 2 * count] + outer[2 * count :]

        def around(value, k):
            total = outer[k * chans : (k + 1) * chans]
            total = total + jnp.where(lane < side, 0.0, pltpu.roll(value, side, 1))
            total = total + jnp.where(
                lane >= pixels - side, 0.0, pltpu.roll(value, pixels - side, 1)
            )
            total = total + jnp.where(y_at == 0, 0.0, pltpu.roll(value, 1, 1))
            return total + jnp.where(y_at == side - 1, 0.0, pltpu.roll(value, pixels - 1, 1))

        previous, current = own[m], -0.25 * around(own[m], 0)
        held = [previous]
        for k in range(1, K):
            high = current.astype(jnp.bfloat16).astype(jnp.float32)
            held += [high, current - high]
            if k < K - 1:
                previous, current = current, -0.5 * around(current, k) - previous
        term = jnp.concatenate(held, axis=0).astype(jnp.bfloat16)
        terms.append(term)
        mixed = jnp.dot(mixing, term, preferred_element_type=jnp.float32)
        for e in range(subs):
            part[m, e] = mixed[e * chans : (e + 1) * chans]
        for d, peer in enumerate(sub_peers):
            part_copy(m, d, s, peer).start()

    x_all[s] = x_ref[...]
    for d, peer in enumerate(sub_peers):
        x_copy(d, peer, peer).wait_recv()
    for m in range(slots):
        maps = jnp.concatenate(
            [x_all[e, slot_list[m]].astype(jnp.float32) for e in range(subs)], axis=0
        ).astype(jnp.bfloat16)
        grad = grad + lax.dot_general(
            maps, terms[m], (((1,), (1,)), ((), ())), preferred_element_type=jnp.float32
        )
    sums = [grad[:, :chans]]
    for k in range(1, K):
        at = (2 * k - 1) * chans
        sums.append(grad[:, at : at + chans] + grad[:, at + chans : at + 2 * chans])
    sums.append(jnp.zeros((subs * chans, block.shape[2] - K * chans), jnp.float32))
    blocks = jnp.concatenate(sums, axis=1) * scale
    for e in range(subs):
        block[e] = blocks[e * chans : (e + 1) * chans]
    me = j * subs + s
    for order, (d, e) in enumerate(every):
        block_copy(order, d, e, me).start()
    block_in[me] = block[s]

    for m in range(slots):
        for d, peer in enumerate(sub_peers):
            part_copy(m, d, peer, peer).wait_recv()
        part_in[m, s] = part[m, s]
    for slot in range(slots):
        m = lax.rem(map_ref[base + slot], slots)
        total = part_in[m, 0]
        for e in range(1, subs):
            total = total + part_in[m, e]
        in_ref[slot] = total.astype(in_ref.dtype)

    for order, (d, e) in enumerate(every):
        sender = lax.rem(j + d, tiles_n) * subs + lax.rem(s + e, subs)
        block_copy(order, d, e, sender).wait_recv()
    whole = []
    for e in range(subs):
        total = block_in[e]
        for t in range(1, tiles_n):
            total = total + block_in[t * subs + e]
        whole.append(total)
    for k in range(K):
        w_ref[k] = jnp.concatenate([v[:, k * chans : (k + 1) * chans] for v in whole], axis=1)

    for d, peer in enumerate(tile_peers):
        strip_copy(d, j, peer).wait_send()
    for d, peer in enumerate(sub_peers):
        x_copy(d, s, peer).wait_send()
        for m in range(slots):
            part_copy(m, d, s, peer).wait_send()
    for order, (d, e) in enumerate(every):
        block_copy(order, d, e, me).wait_send()


def face_path(features, out_grad, filters, tile_map):
    slots, chans, pixels = features.shape
    side = math.isqrt(pixels)
    tiles_n, subs = lax.axis_size("tile"), lax.axis_size("sub")
    matrices, table, spread, take = ghost_tables(side)
    scale = 1.0 / math.sqrt(slots * tiles_n * pixels)
    width = DEPTH * side
    vmem = pl.BlockSpec(memory_space=pltpu.VMEM)
    smem = pl.BlockSpec(memory_space=pltpu.SMEM)
    hbm = pl.BlockSpec(memory_space=pl.ANY)
    dma = pltpu.SemaphoreType.DMA
    return pl.pallas_call(
        functools.partial(face_kernel, (slots, tiles_n, subs, side, scale)),
        out_shape=(
            jax.ShapeDtypeStruct(features.shape, jnp.bfloat16),
            jax.ShapeDtypeStruct((K, chans, filters.shape[2]), jnp.float32),
        ),
        in_specs=[vmem, vmem, vmem, smem, smem, hbm, hbm, hbm],
        out_specs=(vmem, vmem),
        scratch_shapes=[
            pltpu.VMEM((slots * tiles_n * 4, chans, width), jnp.bfloat16),
            pltpu.VMEM((subs,) + features.shape, jnp.bfloat16),
            pltpu.VMEM((slots, subs, chans, pixels), jnp.float32),
            pltpu.VMEM((slots, subs, chans, pixels), jnp.float32),
            pltpu.VMEM((subs, chans, 128), jnp.float32),
            pltpu.VMEM((subs * tiles_n, chans, 128), jnp.float32),
            pltpu.VMEM((slots,) + matrices.shape[1:], jnp.int8),
            pltpu.VMEM((slots,) + matrices.shape[1:], jnp.bfloat16),
            pltpu.VMEM(spread.shape, jnp.bfloat16),
            pltpu.VMEM(take.shape, jnp.bfloat16),
            dma((2 + slots,)),
            dma((tiles_n,)),
            dma((tiles_n,)),
            dma((subs,)),
            dma((subs,)),
            dma((slots, subs)),
            dma((slots, subs)),
            dma((subs * tiles_n,)),
            dma((subs * tiles_n,)),
        ],
        compiler_params=pltpu.CompilerParams(
            collective_id=0, has_side_effects=True, vmem_limit_bytes=40 * 2**20
        ),
    )(
        features,
        out_grad,
        filters,
        tile_map,
        jnp.asarray(table),
        jnp.asarray(matrices),
        jnp.asarray(spread, jnp.bfloat16),
        jnp.asarray(take, jnp.bfloat16),
    )


def on_device(features, out_grad, filters, tile_map):
    slots, chans, pixels = features.shape
    side = math.isqrt(pixels)
    whole_faces = slots * lax.axis_size("tile") == 12
    if whole_faces and DEPTH * side == 128 and chans % 8 == 0 and K * chans <= 128:
        return face_path(features, out_grad, filters, tile_map)
    return general_path(features, out_grad, filters, tile_map)


def solution(mesh):
    placed = (P(("grp", "tile"), "sub", None), P(("grp", "tile"), "sub", None), P(), P())
    return jax.shard_map(
        on_device,
        mesh=mesh,
        in_specs=placed,
        out_specs=(P(("grp", "tile"), "sub", None), P("grp", "sub", None)),
        check_vma=False,
    )
```

```python
import functools
import math

import jax
import jax.numpy as jnp
import numpy as np
from jax import lax
from jax.experimental import pallas as pl
from jax.experimental.pallas import tpu as pltpu
from jax.sharding import PartitionSpec as P

K = 5


def from_behind(value, axis, steps):
    count = lax.axis_size(axis)
    pairs = [(source, (source + steps) % count) for source in range(count)]
    return lax.ppermute(value, axis, pairs)


def tile_coords(nested_code, bit_count):
    coord_x = nested_code * 0
    coord_y = nested_code * 0
    for bit_level in range(bit_count):
        coord_x = coord_x + nested_code // 4**bit_level % 2 * 2**bit_level
        coord_y = coord_y + nested_code // (2 * 4**bit_level) % 2 * 2**bit_level
    return (coord_x, coord_y)


def nested_index(coord_x, coord_y, bit_count):
    nested_code = coord_x * 0
    for bit_level in range(bit_count):
        nested_code = nested_code + coord_x // 2**bit_level % 2 * 4**bit_level
        nested_code = nested_code + coord_y // 2**bit_level % 2 * (2 * 4**bit_level)
    return nested_code


def pick(condition, when_true, when_false):
    return when_false + (when_true - when_false) * condition


def neighbour_codes(tile_ids, per_face, side_count):
    bit_count = side_count.bit_length() - 1
    face_id = tile_ids // per_face
    coord_x, coord_y = tile_coords(tile_ids % per_face, bit_count)
    column = face_id % 4
    is_north = face_id < 4
    is_south = face_id >= 8
    last_tile = side_count - 1

    def by_cycle(north_value, equator_value, south_value):
        return pick(is_north, north_value, pick(is_south, south_value, equator_value))

    side_rules = [
        (
            coord_x > 0,
            (face_id, coord_x - 1, coord_y, 1),
            (
                by_cycle(4 + column, 8 + (column + 3) % 4, 8 + (column + 3) % 4),
                by_cycle(last_tile, last_tile, coord_y),
                by_cycle(coord_y, coord_y, 0),
                by_cycle(1, 1, 2),
            ),
        ),
        (
            coord_x < last_tile,
            (face_id, coord_x + 1, coord_y, 0),
            (
                by_cycle((column + 1) % 4, column, 4 + (column + 1) % 4),
                by_cycle(coord_y, 0, 0),
                by_cycle(last_tile, coord_y, coord_y),
                by_cycle(3, 0, 0),
            ),
        ),
        (
            coord_y > 0,
            (face_id, coord_x, coord_y - 1, 3),
            (
                by_cycle(4 + (column + 1) % 4, 8 + column, 8 + (column + 1) % 4),
                by_cycle(coord_x, coord_x, 0),
                by_cycle(last_tile, last_tile, coord_x),
                by_cycle(3, 3, 0),
            ),
        ),
        (
            coord_y < last_tile,
            (face_id, coord_x, coord_y + 1, 2),
            (
                by_cycle((column + 3) % 4, (column + 3) % 4, 4 + column),
                by_cycle(last_tile, coord_x, coord_x),
                by_cycle(coord_x, 0, 0),
                by_cycle(1, 2, 2),
            ),
        ),
    ]
    target_list = []
    edge_list = []
    for inside, within, across in side_rules:
        chosen = [
            pick(inside, near_value, far_value) for near_value, far_value in zip(within, across)
        ]
        target_list.append(chosen[0] * per_face + nested_index(chosen[1], chosen[2], bit_count))
        edge_list.append(chosen[3] + tile_ids * 0)
    return (target_list, edge_list)


def neighbour_table(tile_map, per_face, side_count):
    target_list, edge_list = neighbour_codes(tile_map, per_face, side_count)
    targets = jnp.stack(target_list, axis=1).astype(jnp.int32)
    edges = jnp.stack(edge_list, axis=1).astype(jnp.int32)
    slot_of = jnp.argsort(tile_map).astype(jnp.int32)
    return (slot_of[targets].astype(jnp.int32), edges)


def peer_offsets(slot_count, device_count, per_face, side_count):
    tile_ids = np.arange(slot_count * device_count, dtype=np.int64)
    target_list, edge_list = neighbour_codes(tile_ids, per_face, side_count)
    targets = np.stack(target_list, axis=1)
    offsets = (tile_ids[:, None] // slot_count - targets // slot_count) % device_count
    distinct = sorted(set((int(value) for value in offsets.ravel())) - {0})
    position = np.zeros(device_count, dtype=np.int32)
    for order, value in enumerate(distinct):
        position[value] = order + 1
    return (distinct, position)


def edge_lines(values, tile_side):
    return jnp.stack(
        [
            values[..., :tile_side],
            values[..., -tile_side:],
            values[..., ::tile_side],
            values[..., tile_side - 1 :: tile_side],
        ],
        axis=1,
    )


def stencil(values, ghosts, tile_side):
    position = jnp.arange(values.shape[-1]) % tile_side
    zero_line = jnp.zeros_like(values[..., :1])
    upper_side = jnp.concatenate([ghosts[:, 0], values[..., :-tile_side]], axis=-1)
    lower_side = jnp.concatenate([values[..., tile_side:], ghosts[:, 1]], axis=-1)
    left_side = jnp.where(
        position == 0,
        jnp.repeat(ghosts[:, 2], tile_side, axis=-1),
        jnp.concatenate([zero_line, values[..., :-1]], axis=-1),
    )
    right_side = jnp.where(
        position == tile_side - 1,
        jnp.repeat(ghosts[:, 3], tile_side, axis=-1),
        jnp.concatenate([values[..., 1:], zero_line], axis=-1),
    )
    return -0.25 * (upper_side + lower_side + left_side + right_side)


def tile_total(filter_part):
    return lax.psum(filter_part, "tile")


def general_path(features, out_grad, filters, tile_map):
    slot_count = features.shape[0]
    group_channels = features.shape[1]
    tile_side = math.isqrt(features.shape[2])
    device_count = lax.axis_size("tile")
    total_tiles = slot_count * device_count
    side_count = math.isqrt(total_tiles // 12)
    scale_factor = 1.0 / math.sqrt(total_tiles * features.shape[2])
    highest = lax.Precision.HIGHEST
    slot_table, edge_table = neighbour_table(tile_map, total_tiles // 12, side_count)
    my_device = lax.axis_index("tile")
    first_slot = my_device * slot_count
    my_slots = lax.dynamic_slice_in_dim(slot_table, first_slot, slot_count, 0)
    my_edges = lax.dynamic_slice_in_dim(edge_table, first_slot, slot_count, 0)
    channel_start = lax.axis_index("sub") * group_channels
    weights = filters.astype(jnp.float32)
    distinct, position = peer_offsets(slot_count, device_count, total_tiles // 12, side_count)
    sender_gap = (my_device - my_slots // slot_count) % device_count
    local_rows = jnp.asarray(position)[sender_gap] * slot_count + my_slots % slot_count

    def laplace(values):
        border = edge_lines(values, tile_side).reshape(slot_count, 4, group_channels * tile_side)
        received = [border]
        for offset_value in distinct:
            received.append(from_behind(border, "tile", offset_value))
        stacked = jnp.concatenate(received, axis=0)
        stacked = stacked.reshape(stacked.shape[0], 4, group_channels, tile_side)
        ghosts = stacked[local_rows, my_edges]
        return stencil(values, ghosts, tile_side)

    whole_grad = lax.all_gather(out_grad, "sub", axis=1, tiled=True)
    cotangent = whole_grad.astype(jnp.float32)
    inputs = features.astype(jnp.float32)
    previous, current = (inputs, laplace(inputs))
    filter_terms = [
        jnp.einsum("sip,sop->io", inputs, cotangent, precision=highest),
        jnp.einsum("sip,sop->io", current, cotangent, precision=highest),
    ]
    for degree in range(2, K):
        previous, current = (current, 2.0 * laplace(current) - previous)
        filter_terms.append(jnp.einsum("sip,sop->io", current, cotangent, precision=highest))
    weight_grad = tile_total(jnp.stack(filter_terms)) * scale_factor
    row_block = lax.dynamic_slice_in_dim(weights, channel_start, group_channels, 1)

    def mixed(degree):
        return jnp.einsum("sop,io->sip", cotangent, row_block[degree], precision=highest)

    next_sum = mixed(K - 1)
    after_next = jnp.zeros_like(next_sum)
    for degree in range(K - 2, 0, -1):
        next_sum, after_next = (mixed(degree) + 2.0 * laplace(next_sum) - after_next, next_sum)
    in_grad = (mixed(0) + laplace(next_sum) - after_next).astype(jnp.bfloat16)
    return (in_grad, weight_grad)


DEPTH = K - 1
GHOST_SIDES = (0, 2, 3, 1)


def face_graph(tile_side):
    tile_ids = np.arange(12, dtype=np.int64)
    target_list, edge_list = neighbour_codes(tile_ids, 1, 1)
    targets = np.stack(target_list, axis=1)
    edges = np.stack(edge_list, axis=1)
    pixels = tile_side * tile_side
    grid = np.arange(pixels).reshape(tile_side, tile_side)
    lines = [grid[0], grid[-1], grid[:, 0], grid[:, -1]]
    ghosts = np.zeros((12, 4, tile_side), dtype=np.int64)
    around = np.zeros((12, 4, tile_side, tile_side), dtype=np.int64)
    for tile in range(12):
        for side in range(4):
            ghosts[tile, side] = targets[tile, side] * pixels + lines[edges[tile, side]]
        whole = tile * pixels + grid
        around[tile, 0] = np.concatenate([ghosts[tile, 0][None], whole[:-1]], 0)
        around[tile, 1] = np.concatenate([whole[1:], ghosts[tile, 1][None]], 0)
        around[tile, 2] = np.concatenate([ghosts[tile, 2][:, None], whole[:, :-1]], 1)
        around[tile, 3] = np.concatenate([whole[:, 1:], ghosts[tile, 3][:, None]], 1)
    around = around.transpose(0, 2, 3, 1).reshape(12 * pixels, 4)
    return targets, edges, ghosts, around


@functools.lru_cache(None)
def ghost_tables(tile_side):
    targets, edges, ghosts, around = face_graph(tile_side)
    pixels = tile_side * tile_side
    grid = np.arange(pixels).reshape(tile_side, tile_side)
    strips = np.stack(
        [
            grid[:DEPTH].ravel(),
            grid[-DEPTH:].ravel(),
            grid[:, :DEPTH].T.ravel(),
            grid[:, -DEPTH:].T.ravel(),
        ]
    )
    table = np.zeros((12, 10), dtype=np.int32)
    by_class = []
    for tile in range(12):
        wanted = np.concatenate([ghosts[tile, side] for side in GHOST_SIDES])
        power = np.zeros((wanted.size, 12 * pixels), dtype=np.int32)
        power[np.arange(wanted.size), wanted] = 1
        powers = [power]
        for _ in range(DEPTH - 1):
            powers.append(sum(powers[-1][:, around[:, side]] for side in range(4)))
        rows = np.concatenate(
            [powers[0], powers[1], powers[2] - 8 * powers[0], powers[3] - 12 * powers[1]]
        )
        support = np.flatnonzero(np.any(rows != 0, axis=0))
        sources = [(int(targets[tile, side]), int(edges[tile, side])) for side in range(4)]
        sources += [(tile, side) for side in range(4)]
        covered = set(int(t) * pixels + int(p) for t, e in sources for p in strips[e])
        left = [int(p) for p in support if int(p) not in covered]
        corner_tiles = {}
        for pixel in left:
            corner_tiles.setdefault(pixel // pixels, []).append(pixel % pixels)
        first = lambda t: int(
            np.flatnonzero(np.any(rows[:, [t * pixels + p for p in corner_tiles[t]]] != 0, axis=1))[0]
        )
        for other in sorted(corner_tiles, key=first):
            choice = [e for e in range(4) if set(corner_tiles[other]) <= set(strips[e].tolist())]
            sources.append((other, choice[0]))
        assert len(sources) <= 10
        while len(sources) < 10:
            sources.append(sources[-1])
        table[tile] = [t * 4 + e for t, e in sources]
        lanes = np.concatenate([t * pixels + strips[e] for t, e in sources])
        seen, keep = set(), np.zeros(lanes.size, dtype=bool)
        for lane, pixel in enumerate(lanes.tolist()):
            keep[lane] = pixel not in seen
            seen.add(pixel)
        assert set(support.tolist()) <= seen
        matrix = (rows[:, lanes] * keep[None]).T
        assert np.abs(matrix).max() <= 127
        if tile % 4 == 0:
            by_class.append(matrix)
        else:
            assert np.array_equal(matrix, by_class[-1])
    spread = np.zeros((4, tile_side, tile_side, tile_side), dtype=np.float32)
    step = np.arange(tile_side)
    spread[0, step, 0, step] = 1
    spread[1, step, step, 0] = 1
    spread[2, step, step, -1] = 1
    spread[3, step, -1, step] = 1
    spread = spread.reshape(4 * tile_side, pixels)
    take = np.zeros((pixels, 2 * DEPTH * tile_side), dtype=np.float32)
    take[np.concatenate([strips[2], strips[3]]), np.arange(2 * DEPTH * tile_side)] = 1
    return np.stack(by_class).astype(np.int8), table.reshape(-1), spread, take


def face_kernel(
    sizes,
    x_hbm,
    g_hbm,
    f_hbm,
    map_hbm,
    table_hbm,
    ghost_hbm,
    spread_hbm,
    take_hbm,
    in_ref,
    w_ref,
    strips,
    x_all,
    part,
    part_in,
    block,
    block_in,
    ghost_raw,
    ghost,
    spread,
    take,
    g_ref,
    f_ref,
    map_ref,
    table_ref,
    load_sem,
    s_send,
    s_recv,
    x_send,
    x_recv,
    p_send,
    p_recv,
    w_send,
    w_recv,
):
    slots, tiles_n, subs, side, scale = sizes
    chans = g_ref.shape[1]
    pixels = side * side
    width = DEPTH * side
    j = lax.axis_index("tile")
    s = lax.axis_index("sub")
    tile_peers = [lax.rem(j + d, tiles_n) for d in range(1, tiles_n)]
    sub_peers = [lax.rem(s + d, subs) for d in range(1, subs)]
    every = [(d, e) for d in range(tiles_n) for e in range(subs) if d + e > 0]

    def device(d, e):
        return {"tile": lax.rem(j + d, tiles_n), "sub": lax.rem(s + e, subs)}

    slot_loads = [
        pltpu.make_async_copy(map_hbm, map_ref, load_sem.at[0]),
        pltpu.make_async_copy(g_hbm, g_ref, load_sem.at[1]),
        pltpu.make_async_copy(take_hbm, take, load_sem.at[2]),
    ]
    for copy in slot_loads:
        copy.start()
    barrier = pltpu.get_barrier_semaphore()
    for d, e in every:
        pl.semaphore_signal(
            barrier, inc=1, device_id=device(d, e), device_id_type=pl.DeviceIdType.MESH
        )
    loads = [
        pltpu.make_async_copy(f_hbm, f_ref, load_sem.at[3]),
        pltpu.make_async_copy(table_hbm, table_ref, load_sem.at[4]),
        pltpu.make_async_copy(spread_hbm, spread, load_sem.at[5]),
        pltpu.make_async_copy(x_hbm, x_all.at[s], load_sem.at[6]),
    ]
    for m in range(slots):
        kind = (slots * j + m) // 4
        loads.append(
            pltpu.make_async_copy(ghost_hbm.at[kind], ghost_raw.at[m], load_sem.at[7 + m])
        )
    for copy in loads:
        copy.start()

    base = slots * j
    for copy in slot_loads:
        copy.wait()

    def slot_of(m):
        found = 0
        for slot in range(1, slots):
            found = jnp.where(map_ref[base + slot] == base + m, slot, found)
        return found

    slot_list = [slot_of(m) for m in range(slots)]
    own = [g_ref[slot_list[m]].astype(jnp.float32) for m in range(slots)]
    stacked = jnp.concatenate(own, axis=0).astype(jnp.bfloat16)
    cut = jnp.dot(stacked, take[...], preferred_element_type=jnp.float32)
    for m in range(slots):
        rows = slice(m * chans, (m + 1) * chans)
        row = (base + m) * 4
        strips[row] = own[m][:, :width].astype(jnp.bfloat16)
        strips[row + 1] = own[m][:, pixels - width :].astype(jnp.bfloat16)
        strips[row + 2] = cut[rows, :width].astype(jnp.bfloat16)
        strips[row + 3] = cut[rows, width:].astype(jnp.bfloat16)
    pl.semaphore_wait(barrier, len(every))

    def strip_copy(d, sender, target):
        mine = strips.at[pl.ds(sender * slots * 4, slots * 4)]
        return pltpu.make_async_remote_copy(
            mine,
            mine,
            s_send.at[d],
            s_recv.at[sender],
            device_id={"tile": target},
            device_id_type=pl.DeviceIdType.MESH,
        )

    def x_copy(d, sender, target):
        return pltpu.make_async_remote_copy(
            x_hbm,
            x_all.at[sender],
            x_send.at[d],
            x_recv.at[sender],
            device_id={"sub": target},
            device_id_type=pl.DeviceIdType.MESH,
        )

    def part_copy(m, d, sender, target):
        return pltpu.make_async_remote_copy(
            part.at[m, target],
            part_in.at[m, sender],
            p_send.at[m, d],
            p_recv.at[m, sender],
            device_id={"sub": target},
            device_id_type=pl.DeviceIdType.MESH,
        )

    def block_copy(order, d, e, sender):
        return pltpu.make_async_remote_copy(
            block.at[lax.rem(s + e, subs)],
            block_in.at[sender],
            w_send.at[order],
            w_recv.at[sender],
            device_id=device(d, e),
            device_id_type=pl.DeviceIdType.MESH,
        )

    for d, peer in enumerate(tile_peers):
        strip_copy(d, j, peer).start()
    for d, peer in enumerate(sub_peers):
        x_copy(d, s, peer).start()

    loads[0].wait()
    total_rows = (2 * K - 1) * chans
    row_k = lax.broadcasted_iota(jnp.int32, (subs * chans, total_rows), 1) // chans
    row_o = lax.broadcasted_iota(jnp.int32, (subs * chans, total_rows), 1) % chans
    from_o = lax.broadcasted_iota(jnp.int32, (subs * chans, total_rows), 0)
    mine_o = from_o == row_o + chans * s
    mixing = jnp.zeros((subs * chans, total_rows), jnp.float32)
    for k in range(K):
        chosen = jnp.where(mine_o & ((row_k + 1) // 2 == k), 1.0, 0.0).astype(jnp.bfloat16)
        mixing = mixing + jnp.dot(f_ref[k], chosen, preferred_element_type=jnp.float32)
    mixing = mixing.astype(jnp.bfloat16)

    for copy in loads[1:]:
        copy.wait()
    chunk = 128

    def widen(step, carry):
        at = pl.ds(pl.multiple_of(step * chunk, chunk), chunk)
        for m in range(slots):
            ghost[m, at, :] = ghost_raw[m, at, :].astype(jnp.float32).astype(jnp.bfloat16)
        return carry

    lax.fori_loop(0, ghost.shape[1] // chunk, widen, 0)

    for d, peer in enumerate(tile_peers):
        strip_copy(d, peer, peer).wait_recv()
    lane = lax.broadcasted_iota(jnp.int32, (chans, pixels), 1)
    y_at = lane % side
    scales = (1.0, -0.25, 0.125, -0.0625)
    grad = jnp.zeros((subs * chans, total_rows), jnp.float32)
    terms = []
    for m in range(slots):
        pieces = [
            strips[table_ref[(base + m) * 10 + r]].astype(jnp.float32) for r in range(10)
        ]
        source = jnp.concatenate(pieces, axis=1).astype(jnp.bfloat16)
        lines = jnp.dot(source, ghost[m], preferred_element_type=jnp.float32)
        lines = jnp.concatenate(
            [lines[:, k * 4 * side : (k + 1) * 4 * side] * scales[k] for k in range(DEPTH)], axis=0
        )
        high = lines.astype(jnp.bfloat16).astype(jnp.float32)
        rest = lines - high
        middle = rest.astype(jnp.bfloat16).astype(jnp.float32)
        split = jnp.concatenate([high, middle, rest - middle], axis=0).astype(jnp.bfloat16)
        outer = jnp.dot(split, spread[...], preferred_element_type=jnp.float32)
        count = DEPTH * chans
        outer = outer[:count] + outer[count : 2 * count] + outer[2 * count :]

        def around(value, k):
            total = outer[k * chans : (k + 1) * chans]
            total = total + jnp.where(lane < side, 0.0, pltpu.roll(value, side, 1))
            total = total + jnp.where(
                lane >= pixels - side, 0.0, pltpu.roll(value, pixels - side, 1)
            )
            total = total + jnp.where(y_at == 0, 0.0, pltpu.roll(value, 1, 1))
            return total + jnp.where(y_at == side - 1, 0.0, pltpu.roll(value, pixels - 1, 1))

        previous, current = own[m], -0.25 * around(own[m], 0)
        held = [previous]
        for k in range(1, K):
            high = current.astype(jnp.bfloat16).astype(jnp.float32)
            held += [high, current - high]
            if k < K - 1:
                previous, current = current, -0.5 * around(current, k) - previous
        term = jnp.concatenate(held, axis=0).astype(jnp.bfloat16)
        terms.append(term)
        mixed = jnp.dot(mixing, term, preferred_element_type=jnp.float32)
        for e in range(subs):
            part[m, e] = mixed[e * chans : (e + 1) * chans]
        for d, peer in enumerate(sub_peers):
            part_copy(m, d, s, peer).start()

    for d, peer in enumerate(sub_peers):
        x_copy(d, peer, peer).wait_recv()
    for m in range(slots):
        maps = jnp.concatenate(
            [x_all[e, slot_list[m]].astype(jnp.float32) for e in range(subs)], axis=0
        ).astype(jnp.bfloat16)
        grad = grad + lax.dot_general(
            maps, terms[m], (((1,), (1,)), ((), ())), preferred_element_type=jnp.float32
        )
    sums = [grad[:, :chans]]
    for k in range(1, K):
        at = (2 * k - 1) * chans
        sums.append(grad[:, at : at + chans] + grad[:, at + chans : at + 2 * chans])
    sums.append(jnp.zeros((subs * chans, block.shape[2] - K * chans), jnp.float32))
    blocks = jnp.concatenate(sums, axis=1) * scale
    for e in range(subs):
        block[e] = blocks[e * chans : (e + 1) * chans]
    me = j * subs + s
    for order, (d, e) in enumerate(every):
        block_copy(order, d, e, me).start()
    block_in[me] = block[s]

    for m in range(slots):
        for d, peer in enumerate(sub_peers):
            part_copy(m, d, peer, peer).wait_recv()
        part_in[m, s] = part[m, s]
    for slot in range(slots):
        m = lax.rem(map_ref[base + slot], slots)
        total = part_in[m, 0]
        for e in range(1, subs):
            total = total + part_in[m, e]
        in_ref[slot] = total.astype(in_ref.dtype)

    for order, (d, e) in enumerate(every):
        sender = lax.rem(j + d, tiles_n) * subs + lax.rem(s + e, subs)
        block_copy(order, d, e, sender).wait_recv()
    whole = []
    for e in range(subs):
        total = block_in[e]
        for t in range(1, tiles_n):
            total = total + block_in[t * subs + e]
        whole.append(total)
    for k in range(K):
        w_ref[k] = jnp.concatenate([v[:, k * chans : (k + 1) * chans] for v in whole], axis=1)

    for d, peer in enumerate(tile_peers):
        strip_copy(d, j, peer).wait_send()
    for d, peer in enumerate(sub_peers):
        x_copy(d, s, peer).wait_send()
        for m in range(slots):
            part_copy(m, d, s, peer).wait_send()
    for order, (d, e) in enumerate(every):
        block_copy(order, d, e, me).wait_send()


def face_path(features, out_grad, filters, tile_map):
    slots, chans, pixels = features.shape
    side = math.isqrt(pixels)
    tiles_n, subs = lax.axis_size("tile"), lax.axis_size("sub")
    matrices, table, spread, take = ghost_tables(side)
    scale = 1.0 / math.sqrt(slots * tiles_n * pixels)
    width = DEPTH * side
    vmem = pl.BlockSpec(memory_space=pltpu.VMEM)
    hbm = pl.BlockSpec(memory_space=pltpu.HBM)
    dma = pltpu.SemaphoreType.DMA
    return pl.pallas_call(
        functools.partial(face_kernel, (slots, tiles_n, subs, side, scale)),
        out_shape=(
            jax.ShapeDtypeStruct(features.shape, jnp.bfloat16),
            jax.ShapeDtypeStruct((K, chans, filters.shape[2]), jnp.float32),
        ),
        in_specs=[hbm] * 8,
        out_specs=(vmem, vmem),
        scratch_shapes=[
            pltpu.VMEM((slots * tiles_n * 4, chans, width), jnp.bfloat16),
            pltpu.VMEM((subs,) + features.shape, jnp.bfloat16),
            pltpu.VMEM((slots, subs, chans, pixels), jnp.float32),
            pltpu.VMEM((slots, subs, chans, pixels), jnp.float32),
            pltpu.VMEM((subs, chans, 128), jnp.float32),
            pltpu.VMEM((subs * tiles_n, chans, 128), jnp.float32),
            pltpu.VMEM((slots,) + matrices.shape[1:], jnp.int8),
            pltpu.VMEM((slots,) + matrices.shape[1:], jnp.bfloat16),
            pltpu.VMEM(spread.shape, jnp.bfloat16),
            pltpu.VMEM(take.shape, jnp.bfloat16),
            pltpu.VMEM(features.shape, jnp.bfloat16),
            pltpu.VMEM(filters.shape, jnp.bfloat16),
            pltpu.SMEM(tile_map.shape, jnp.int32),
            pltpu.SMEM(table.shape, jnp.int32),
            dma((7 + slots,)),
            dma((tiles_n,)),
            dma((tiles_n,)),
            dma((subs,)),
            dma((subs,)),
            dma((slots, subs)),
            dma((slots, subs)),
            dma((subs * tiles_n,)),
            dma((subs * tiles_n,)),
        ],
        compiler_params=pltpu.CompilerParams(
            collective_id=0, has_side_effects=True, vmem_limit_bytes=67043328
        ),
    )(
        features,
        out_grad,
        filters,
        tile_map,
        jnp.asarray(table),
        jnp.asarray(matrices),
        jnp.asarray(spread, jnp.bfloat16),
        jnp.asarray(take, jnp.bfloat16),
    )


def on_device(features, out_grad, filters, tile_map):
    slots, chans, pixels = features.shape
    side = math.isqrt(pixels)
    whole_faces = slots * lax.axis_size("tile") == 12
    if whole_faces and DEPTH * side == 128 and chans % 8 == 0 and K * chans <= 128:
        return face_path(features, out_grad, filters, tile_map)
    return general_path(features, out_grad, filters, tile_map)


def solution(mesh):
    placed = (P(("grp", "tile"), "sub", None), P(("grp", "tile"), "sub", None), P(), P())
    return jax.shard_map(
        on_device,
        mesh=mesh,
        in_specs=placed,
        out_specs=(P(("grp", "tile"), "sub", None), P("grp", "sub", None)),
        check_vma=False,
    )
```

```python
import functools
import math

import jax
import jax.numpy as jnp
import numpy as np
from jax import lax
from jax.experimental import pallas as pl
from jax.experimental.pallas import tpu as pltpu
from jax.sharding import PartitionSpec as P

K = 5


def from_behind(value, axis, steps):
    count = lax.axis_size(axis)
    pairs = [(source, (source + steps) % count) for source in range(count)]
    return lax.ppermute(value, axis, pairs)


def tile_coords(nested_code, bit_count):
    coord_x = nested_code * 0
    coord_y = nested_code * 0
    for bit_level in range(bit_count):
        coord_x = coord_x + nested_code // 4**bit_level % 2 * 2**bit_level
        coord_y = coord_y + nested_code // (2 * 4**bit_level) % 2 * 2**bit_level
    return (coord_x, coord_y)


def nested_index(coord_x, coord_y, bit_count):
    nested_code = coord_x * 0
    for bit_level in range(bit_count):
        nested_code = nested_code + coord_x // 2**bit_level % 2 * 4**bit_level
        nested_code = nested_code + coord_y // 2**bit_level % 2 * (2 * 4**bit_level)
    return nested_code


def pick(condition, when_true, when_false):
    return when_false + (when_true - when_false) * condition


def neighbour_codes(tile_ids, per_face, side_count):
    bit_count = side_count.bit_length() - 1
    face_id = tile_ids // per_face
    coord_x, coord_y = tile_coords(tile_ids % per_face, bit_count)
    column = face_id % 4
    is_north = face_id < 4
    is_south = face_id >= 8
    last_tile = side_count - 1

    def by_cycle(north_value, equator_value, south_value):
        return pick(is_north, north_value, pick(is_south, south_value, equator_value))

    side_rules = [
        (
            coord_x > 0,
            (face_id, coord_x - 1, coord_y, 1),
            (
                by_cycle(4 + column, 8 + (column + 3) % 4, 8 + (column + 3) % 4),
                by_cycle(last_tile, last_tile, coord_y),
                by_cycle(coord_y, coord_y, 0),
                by_cycle(1, 1, 2),
            ),
        ),
        (
            coord_x < last_tile,
            (face_id, coord_x + 1, coord_y, 0),
            (
                by_cycle((column + 1) % 4, column, 4 + (column + 1) % 4),
                by_cycle(coord_y, 0, 0),
                by_cycle(last_tile, coord_y, coord_y),
                by_cycle(3, 0, 0),
            ),
        ),
        (
            coord_y > 0,
            (face_id, coord_x, coord_y - 1, 3),
            (
                by_cycle(4 + (column + 1) % 4, 8 + column, 8 + (column + 1) % 4),
                by_cycle(coord_x, coord_x, 0),
                by_cycle(last_tile, last_tile, coord_x),
                by_cycle(3, 3, 0),
            ),
        ),
        (
            coord_y < last_tile,
            (face_id, coord_x, coord_y + 1, 2),
            (
                by_cycle((column + 3) % 4, (column + 3) % 4, 4 + column),
                by_cycle(last_tile, coord_x, coord_x),
                by_cycle(coord_x, 0, 0),
                by_cycle(1, 2, 2),
            ),
        ),
    ]
    target_list = []
    edge_list = []
    for inside, within, across in side_rules:
        chosen = [
            pick(inside, near_value, far_value) for near_value, far_value in zip(within, across)
        ]
        target_list.append(chosen[0] * per_face + nested_index(chosen[1], chosen[2], bit_count))
        edge_list.append(chosen[3] + tile_ids * 0)
    return (target_list, edge_list)


def neighbour_table(tile_map, per_face, side_count):
    target_list, edge_list = neighbour_codes(tile_map, per_face, side_count)
    targets = jnp.stack(target_list, axis=1).astype(jnp.int32)
    edges = jnp.stack(edge_list, axis=1).astype(jnp.int32)
    slot_of = jnp.argsort(tile_map).astype(jnp.int32)
    return (slot_of[targets].astype(jnp.int32), edges)


def peer_offsets(slot_count, device_count, per_face, side_count):
    tile_ids = np.arange(slot_count * device_count, dtype=np.int64)
    target_list, edge_list = neighbour_codes(tile_ids, per_face, side_count)
    targets = np.stack(target_list, axis=1)
    offsets = (tile_ids[:, None] // slot_count - targets // slot_count) % device_count
    distinct = sorted(set((int(value) for value in offsets.ravel())) - {0})
    position = np.zeros(device_count, dtype=np.int32)
    for order, value in enumerate(distinct):
        position[value] = order + 1
    return (distinct, position)


def edge_lines(values, tile_side):
    return jnp.stack(
        [
            values[..., :tile_side],
            values[..., -tile_side:],
            values[..., ::tile_side],
            values[..., tile_side - 1 :: tile_side],
        ],
        axis=1,
    )


def stencil(values, ghosts, tile_side):
    position = jnp.arange(values.shape[-1]) % tile_side
    zero_line = jnp.zeros_like(values[..., :1])
    upper_side = jnp.concatenate([ghosts[:, 0], values[..., :-tile_side]], axis=-1)
    lower_side = jnp.concatenate([values[..., tile_side:], ghosts[:, 1]], axis=-1)
    left_side = jnp.where(
        position == 0,
        jnp.repeat(ghosts[:, 2], tile_side, axis=-1),
        jnp.concatenate([zero_line, values[..., :-1]], axis=-1),
    )
    right_side = jnp.where(
        position == tile_side - 1,
        jnp.repeat(ghosts[:, 3], tile_side, axis=-1),
        jnp.concatenate([values[..., 1:], zero_line], axis=-1),
    )
    return -0.25 * (upper_side + lower_side + left_side + right_side)


def tile_total(filter_part):
    return lax.psum(filter_part, "tile")


def general_path(features, out_grad, filters, tile_map):
    slot_count = features.shape[0]
    group_channels = features.shape[1]
    tile_side = math.isqrt(features.shape[2])
    device_count = lax.axis_size("tile")
    total_tiles = slot_count * device_count
    side_count = math.isqrt(total_tiles // 12)
    scale_factor = 1.0 / math.sqrt(total_tiles * features.shape[2])
    highest = lax.Precision.HIGHEST
    slot_table, edge_table = neighbour_table(tile_map, total_tiles // 12, side_count)
    my_device = lax.axis_index("tile")
    first_slot = my_device * slot_count
    my_slots = lax.dynamic_slice_in_dim(slot_table, first_slot, slot_count, 0)
    my_edges = lax.dynamic_slice_in_dim(edge_table, first_slot, slot_count, 0)
    channel_start = lax.axis_index("sub") * group_channels
    weights = filters.astype(jnp.float32)
    distinct, position = peer_offsets(slot_count, device_count, total_tiles // 12, side_count)
    sender_gap = (my_device - my_slots // slot_count) % device_count
    local_rows = jnp.asarray(position)[sender_gap] * slot_count + my_slots % slot_count

    def laplace(values):
        border = edge_lines(values, tile_side).reshape(slot_count, 4, group_channels * tile_side)
        received = [border]
        for offset_value in distinct:
            received.append(from_behind(border, "tile", offset_value))
        stacked = jnp.concatenate(received, axis=0)
        stacked = stacked.reshape(stacked.shape[0], 4, group_channels, tile_side)
        ghosts = stacked[local_rows, my_edges]
        return stencil(values, ghosts, tile_side)

    whole_grad = lax.all_gather(out_grad, "sub", axis=1, tiled=True)
    cotangent = whole_grad.astype(jnp.float32)
    inputs = features.astype(jnp.float32)
    previous, current = (inputs, laplace(inputs))
    filter_terms = [
        jnp.einsum("sip,sop->io", inputs, cotangent, precision=highest),
        jnp.einsum("sip,sop->io", current, cotangent, precision=highest),
    ]
    for degree in range(2, K):
        previous, current = (current, 2.0 * laplace(current) - previous)
        filter_terms.append(jnp.einsum("sip,sop->io", current, cotangent, precision=highest))
    weight_grad = tile_total(jnp.stack(filter_terms)) * scale_factor
    row_block = lax.dynamic_slice_in_dim(weights, channel_start, group_channels, 1)

    def mixed(degree):
        return jnp.einsum("sop,io->sip", cotangent, row_block[degree], precision=highest)

    next_sum = mixed(K - 1)
    after_next = jnp.zeros_like(next_sum)
    for degree in range(K - 2, 0, -1):
        next_sum, after_next = (mixed(degree) + 2.0 * laplace(next_sum) - after_next, next_sum)
    in_grad = (mixed(0) + laplace(next_sum) - after_next).astype(jnp.bfloat16)
    return (in_grad, weight_grad)


DEPTH = K - 1
GHOST_SIDES = (0, 2, 3, 1)


def face_graph(tile_side):
    tile_ids = np.arange(12, dtype=np.int64)
    target_list, edge_list = neighbour_codes(tile_ids, 1, 1)
    targets = np.stack(target_list, axis=1)
    edges = np.stack(edge_list, axis=1)
    pixels = tile_side * tile_side
    grid = np.arange(pixels).reshape(tile_side, tile_side)
    lines = [grid[0], grid[-1], grid[:, 0], grid[:, -1]]
    ghosts = np.zeros((12, 4, tile_side), dtype=np.int64)
    around = np.zeros((12, 4, tile_side, tile_side), dtype=np.int64)
    for tile in range(12):
        for side in range(4):
            ghosts[tile, side] = targets[tile, side] * pixels + lines[edges[tile, side]]
        whole = tile * pixels + grid
        around[tile, 0] = np.concatenate([ghosts[tile, 0][None], whole[:-1]], 0)
        around[tile, 1] = np.concatenate([whole[1:], ghosts[tile, 1][None]], 0)
        around[tile, 2] = np.concatenate([ghosts[tile, 2][:, None], whole[:, :-1]], 1)
        around[tile, 3] = np.concatenate([whole[:, 1:], ghosts[tile, 3][:, None]], 1)
    around = around.transpose(0, 2, 3, 1).reshape(12 * pixels, 4)
    return targets, edges, ghosts, around


@functools.lru_cache(None)
def ghost_tables(tile_side):
    targets, edges, ghosts, around = face_graph(tile_side)
    pixels = tile_side * tile_side
    grid = np.arange(pixels).reshape(tile_side, tile_side)
    strips = np.stack(
        [
            grid[:DEPTH].ravel(),
            grid[-DEPTH:].ravel(),
            grid[:, :DEPTH].T.ravel(),
            grid[:, -DEPTH:].T.ravel(),
        ]
    )
    table = np.zeros((12, 10), dtype=np.int32)
    by_class = []
    for tile in range(12):
        wanted = np.concatenate([ghosts[tile, side] for side in GHOST_SIDES])
        power = np.zeros((wanted.size, 12 * pixels), dtype=np.int32)
        power[np.arange(wanted.size), wanted] = 1
        powers = [power]
        for _ in range(DEPTH - 1):
            powers.append(sum(powers[-1][:, around[:, side]] for side in range(4)))
        rows = np.concatenate(
            [powers[0], powers[1], powers[2] - 8 * powers[0], powers[3] - 12 * powers[1]]
        )
        support = np.flatnonzero(np.any(rows != 0, axis=0))
        sources = [(int(targets[tile, side]), int(edges[tile, side])) for side in range(4)]
        sources += [(tile, side) for side in range(4)]
        covered = set(int(t) * pixels + int(p) for t, e in sources for p in strips[e])
        left = [int(p) for p in support if int(p) not in covered]
        corner_tiles = {}
        for pixel in left:
            corner_tiles.setdefault(pixel // pixels, []).append(pixel % pixels)
        first = lambda t: int(
            np.flatnonzero(np.any(rows[:, [t * pixels + p for p in corner_tiles[t]]] != 0, axis=1))[0]
        )
        for other in sorted(corner_tiles, key=first):
            choice = [e for e in range(4) if set(corner_tiles[other]) <= set(strips[e].tolist())]
            sources.append((other, choice[0]))
        assert len(sources) <= 10
        while len(sources) < 10:
            sources.append(sources[-1])
        table[tile] = [t * 4 + e for t, e in sources]
        lanes = np.concatenate([t * pixels + strips[e] for t, e in sources])
        seen, keep = set(), np.zeros(lanes.size, dtype=bool)
        for lane, pixel in enumerate(lanes.tolist()):
            keep[lane] = pixel not in seen
            seen.add(pixel)
        assert set(support.tolist()) <= seen
        matrix = (rows[:, lanes] * keep[None]).T
        assert np.abs(matrix).max() <= 127
        if tile % 4 == 0:
            by_class.append(matrix)
        else:
            assert np.array_equal(matrix, by_class[-1])
    spread = np.zeros((4, tile_side, tile_side, tile_side), dtype=np.float32)
    step = np.arange(tile_side)
    spread[0, step, 0, step] = 1
    spread[1, step, step, 0] = 1
    spread[2, step, step, -1] = 1
    spread[3, step, -1, step] = 1
    spread = spread.reshape(4 * tile_side, pixels)
    take = np.zeros((pixels, 2 * DEPTH * tile_side), dtype=np.float32)
    take[np.concatenate([strips[2], strips[3]]), np.arange(2 * DEPTH * tile_side)] = 1
    return np.stack(by_class).astype(np.int8), table.reshape(-1), spread, take


def face_kernel(
    sizes,
    x_hbm,
    g_hbm,
    f_hbm,
    map_hbm,
    table_hbm,
    ghost_hbm,
    spread_hbm,
    take_hbm,
    in_ref,
    w_ref,
    strips,
    x_all,
    part,
    part_in,
    block,
    block_in,
    summed,
    summed_in,
    ghost_raw,
    ghost,
    spread,
    take,
    g_ref,
    f_ref,
    map_ref,
    table_ref,
    load_sem,
    s_send,
    s_recv,
    x_send,
    x_recv,
    p_send,
    p_recv,
    w_send,
    w_recv,
    t_send,
    t_recv,
):
    slots, tiles_n, subs, side, scale = sizes
    chans = g_ref.shape[1]
    pixels = side * side
    width = DEPTH * side
    j = lax.axis_index("tile")
    s = lax.axis_index("sub")
    tile_peers = []
    for d in range(tiles_n - 1):
        up = d + (j <= d).astype(jnp.int32)
        back = tiles_n - 2 - d
        down = back + (j <= back).astype(jnp.int32)
        tile_peers.append(jnp.where(2 * j < tiles_n, down, up))
    sub_peers = [lax.rem(s + d, subs) for d in range(1, subs)]
    slot_loads = [
        pltpu.make_async_copy(map_hbm, map_ref, load_sem.at[0]),
        pltpu.make_async_copy(g_hbm, g_ref, load_sem.at[1]),
        pltpu.make_async_copy(take_hbm, take, load_sem.at[2]),
    ]
    for copy in slot_loads:
        copy.start()
    barrier = pltpu.get_barrier_semaphore()
    friends = [{"tile": peer} for peer in tile_peers] + [{"sub": peer} for peer in sub_peers]
    for friend in friends:
        pl.semaphore_signal(
            barrier, inc=1, device_id=friend, device_id_type=pl.DeviceIdType.MESH
        )
    loads = [
        pltpu.make_async_copy(f_hbm, f_ref, load_sem.at[3]),
        pltpu.make_async_copy(table_hbm, table_ref, load_sem.at[4]),
        pltpu.make_async_copy(spread_hbm, spread, load_sem.at[5]),
        pltpu.make_async_copy(x_hbm, x_all.at[s], load_sem.at[6]),
    ]
    for m in range(slots):
        kind = (slots * j + m) // 4
        loads.append(
            pltpu.make_async_copy(ghost_hbm.at[kind], ghost_raw.at[m], load_sem.at[7 + m])
        )
    for copy in loads:
        copy.start()

    base = slots * j
    for copy in slot_loads:
        copy.wait()

    def slot_of(m):
        found = 0
        for slot in range(1, slots):
            found = jnp.where(map_ref[base + slot] == base + m, slot, found)
        return found

    slot_list = [slot_of(m) for m in range(slots)]
    own = [g_ref[slot_list[m]].astype(jnp.float32) for m in range(slots)]
    stacked = jnp.concatenate(own, axis=0).astype(jnp.bfloat16)
    cut = jnp.dot(stacked, take[...], preferred_element_type=jnp.float32)
    for m in range(slots):
        rows = slice(m * chans, (m + 1) * chans)
        row = (base + m) * 4
        strips[row] = own[m][:, :width].astype(jnp.bfloat16)
        strips[row + 1] = own[m][:, pixels - width :].astype(jnp.bfloat16)
        strips[row + 2] = cut[rows, :width].astype(jnp.bfloat16)
        strips[row + 3] = cut[rows, width:].astype(jnp.bfloat16)
    pl.semaphore_wait(barrier, len(friends))

    def strip_copy(d, sender, target):
        mine = strips.at[pl.ds(sender * slots * 4, slots * 4)]
        return pltpu.make_async_remote_copy(
            mine,
            mine,
            s_send.at[d],
            s_recv.at[sender],
            device_id={"tile": target},
            device_id_type=pl.DeviceIdType.MESH,
        )

    def x_copy(d, sender, target):
        return pltpu.make_async_remote_copy(
            x_hbm,
            x_all.at[sender],
            x_send.at[d],
            x_recv.at[sender],
            device_id={"sub": target},
            device_id_type=pl.DeviceIdType.MESH,
        )

    def part_copy(m, d, sender, target):
        return pltpu.make_async_remote_copy(
            part.at[m, target],
            part_in.at[m, sender],
            p_send.at[m, d],
            p_recv.at[m, sender],
            device_id={"sub": target},
            device_id_type=pl.DeviceIdType.MESH,
        )

    def block_copy(d, sender, target):
        return pltpu.make_async_remote_copy(
            block,
            block_in.at[sender],
            w_send.at[d],
            w_recv.at[sender],
            device_id={"tile": target},
            device_id_type=pl.DeviceIdType.MESH,
        )

    def sum_copy(d, sender, target):
        return pltpu.make_async_remote_copy(
            summed.at[target],
            summed_in.at[sender],
            t_send.at[d],
            t_recv.at[sender],
            device_id={"sub": target},
            device_id_type=pl.DeviceIdType.MESH,
        )

    for d, peer in enumerate(tile_peers):
        strip_copy(d, j, peer).start()
    for d, peer in enumerate(sub_peers):
        x_copy(d, s, peer).start()

    loads[0].wait()
    total_rows = (2 * K - 1) * chans
    row_k = lax.broadcasted_iota(jnp.int32, (subs * chans, total_rows), 1) // chans
    row_o = lax.broadcasted_iota(jnp.int32, (subs * chans, total_rows), 1) % chans
    from_o = lax.broadcasted_iota(jnp.int32, (subs * chans, total_rows), 0)
    mine_o = from_o == row_o + chans * s
    mixing = jnp.zeros((subs * chans, total_rows), jnp.float32)
    for k in range(K):
        chosen = jnp.where(mine_o & ((row_k + 1) // 2 == k), 1.0, 0.0).astype(jnp.bfloat16)
        mixing = mixing + jnp.dot(f_ref[k], chosen, preferred_element_type=jnp.float32)
    mixing = mixing.astype(jnp.bfloat16)

    for copy in loads[1:]:
        copy.wait()
    chunk = 128

    def widen(step, carry):
        at = pl.ds(pl.multiple_of(step * chunk, chunk), chunk)
        for m in range(slots):
            ghost[m, at, :] = ghost_raw[m, at, :].astype(jnp.float32).astype(jnp.bfloat16)
        return carry

    lax.fori_loop(0, ghost.shape[1] // chunk, widen, 0)

    for d, peer in enumerate(tile_peers):
        strip_copy(d, peer, peer).wait_recv()
    lane = lax.broadcasted_iota(jnp.int32, (chans, pixels), 1)
    y_at = lane % side
    scales = (1.0, -0.25, 0.125, -0.0625)
    grad = jnp.zeros((subs * chans, total_rows), jnp.float32)
    terms = []
    for m in range(slots):
        pieces = [
            strips[table_ref[(base + m) * 10 + r]].astype(jnp.float32) for r in range(10)
        ]
        source = jnp.concatenate(pieces, axis=1).astype(jnp.bfloat16)
        lines = jnp.dot(source, ghost[m], preferred_element_type=jnp.float32)
        lines = jnp.concatenate(
            [lines[:, k * 4 * side : (k + 1) * 4 * side] * scales[k] for k in range(DEPTH)], axis=0
        )
        high = lines.astype(jnp.bfloat16).astype(jnp.float32)
        rest = lines - high
        middle = rest.astype(jnp.bfloat16).astype(jnp.float32)
        split = jnp.concatenate([high, middle, rest - middle], axis=0).astype(jnp.bfloat16)
        outer = jnp.dot(split, spread[...], preferred_element_type=jnp.float32)
        count = DEPTH * chans
        outer = outer[:count] + outer[count : 2 * count] + outer[2 * count :]

        def around(value, k):
            total = outer[k * chans : (k + 1) * chans]
            total = total + jnp.where(lane < side, 0.0, pltpu.roll(value, side, 1))
            total = total + jnp.where(
                lane >= pixels - side, 0.0, pltpu.roll(value, pixels - side, 1)
            )
            total = total + jnp.where(y_at == 0, 0.0, pltpu.roll(value, 1, 1))
            return total + jnp.where(y_at == side - 1, 0.0, pltpu.roll(value, pixels - 1, 1))

        previous, current = own[m], -0.25 * around(own[m], 0)
        held = [previous]
        for k in range(1, K):
            high = current.astype(jnp.bfloat16).astype(jnp.float32)
            held += [high, current - high]
            if k < K - 1:
                previous, current = current, -0.5 * around(current, k) - previous
        term = jnp.concatenate(held, axis=0).astype(jnp.bfloat16)
        terms.append(term)
        mixed = jnp.dot(mixing, term, preferred_element_type=jnp.float32)
        for e in range(subs):
            part[m, e] = mixed[e * chans : (e + 1) * chans]
        for d, peer in enumerate(sub_peers):
            part_copy(m, d, s, peer).start()

    for d, peer in enumerate(sub_peers):
        x_copy(d, peer, peer).wait_recv()
    for m in range(slots):
        maps = jnp.concatenate(
            [x_all[e, slot_list[m]].astype(jnp.float32) for e in range(subs)], axis=0
        ).astype(jnp.bfloat16)
        grad = grad + lax.dot_general(
            maps, terms[m], (((1,), (1,)), ((), ())), preferred_element_type=jnp.float32
        )
    sums = [grad[:, :chans]]
    for k in range(1, K):
        at = (2 * k - 1) * chans
        sums.append(grad[:, at : at + chans] + grad[:, at + chans : at + 2 * chans])
    sums.append(jnp.zeros((subs * chans, block.shape[2] - K * chans), jnp.float32))
    blocks = jnp.concatenate(sums, axis=1) * scale
    for e in range(subs):
        block[e] = blocks[e * chans : (e + 1) * chans]
    for d, peer in enumerate(tile_peers):
        block_copy(d, j, peer).start()
    block_in[j] = block[...]
    for d, peer in enumerate(tile_peers):
        block_copy(d, peer, peer).wait_recv()
    total = block_in[0]
    for t in range(1, tiles_n):
        total = total + block_in[t]
    summed[...] = total
    for d, peer in enumerate(sub_peers):
        sum_copy(d, s, peer).start()
    summed_in[s] = summed[s]

    for m in range(slots):
        for d, peer in enumerate(sub_peers):
            part_copy(m, d, peer, peer).wait_recv()
        part_in[m, s] = part[m, s]
    for slot in range(slots):
        m = lax.rem(map_ref[base + slot], slots)
        total = part_in[m, 0]
        for e in range(1, subs):
            total = total + part_in[m, e]
        in_ref[slot] = total.astype(in_ref.dtype)

    for d, peer in enumerate(sub_peers):
        sum_copy(d, peer, peer).wait_recv()
    for k in range(K):
        at = slice(k * chans, (k + 1) * chans)
        w_ref[k] = jnp.concatenate([summed_in[e][:, at] for e in range(subs)], axis=1)

    for d, peer in enumerate(tile_peers):
        strip_copy(d, j, peer).wait_send()
        block_copy(d, j, peer).wait_send()
    for d, peer in enumerate(sub_peers):
        x_copy(d, s, peer).wait_send()
        for m in range(slots):
            part_copy(m, d, s, peer).wait_send()
        sum_copy(d, s, peer).wait_send()


def face_path(features, out_grad, filters, tile_map):
    slots, chans, pixels = features.shape
    side = math.isqrt(pixels)
    tiles_n, subs = lax.axis_size("tile"), lax.axis_size("sub")
    matrices, table, spread, take = ghost_tables(side)
    scale = 1.0 / math.sqrt(slots * tiles_n * pixels)
    width = DEPTH * side
    vmem = pl.BlockSpec(memory_space=pltpu.VMEM)
    hbm = pl.BlockSpec(memory_space=pltpu.HBM)
    dma = pltpu.SemaphoreType.DMA
    return pl.pallas_call(
        functools.partial(face_kernel, (slots, tiles_n, subs, side, scale)),
        out_shape=(
            jax.ShapeDtypeStruct(features.shape, jnp.bfloat16),
            jax.ShapeDtypeStruct((K, chans, filters.shape[2]), jnp.float32),
        ),
        in_specs=[hbm] * 8,
        out_specs=(vmem, vmem),
        scratch_shapes=[
            pltpu.VMEM((slots * tiles_n * 4, chans, width), jnp.bfloat16),
            pltpu.VMEM((subs,) + features.shape, jnp.bfloat16),
            pltpu.VMEM((slots, subs, chans, pixels), jnp.float32),
            pltpu.VMEM((slots, subs, chans, pixels), jnp.float32),
            pltpu.VMEM((subs, chans, 128), jnp.float32),
            pltpu.VMEM((tiles_n, subs, chans, 128), jnp.float32),
            pltpu.VMEM((subs, chans, 128), jnp.float32),
            pltpu.VMEM((subs, chans, 128), jnp.float32),
            pltpu.VMEM((slots,) + matrices.shape[1:], jnp.int8),
            pltpu.VMEM((slots,) + matrices.shape[1:], jnp.bfloat16),
            pltpu.VMEM(spread.shape, jnp.bfloat16),
            pltpu.VMEM(take.shape, jnp.bfloat16),
            pltpu.VMEM(features.shape, jnp.bfloat16),
            pltpu.VMEM(filters.shape, jnp.bfloat16),
            pltpu.SMEM(tile_map.shape, jnp.int32),
            pltpu.SMEM(table.shape, jnp.int32),
            dma((7 + slots,)),
            dma((tiles_n,)),
            dma((tiles_n,)),
            dma((subs,)),
            dma((subs,)),
            dma((slots, subs)),
            dma((slots, subs)),
            dma((tiles_n,)),
            dma((tiles_n,)),
            dma((subs,)),
            dma((subs,)),
        ],
        compiler_params=pltpu.CompilerParams(
            collective_id=0, has_side_effects=True, vmem_limit_bytes=67043328
        ),
    )(
        features,
        out_grad,
        filters,
        tile_map,
        jnp.asarray(table),
        jnp.asarray(matrices),
        jnp.asarray(spread, jnp.bfloat16),
        jnp.asarray(take, jnp.bfloat16),
    )


def on_device(features, out_grad, filters, tile_map):
    slots, chans, pixels = features.shape
    side = math.isqrt(pixels)
    whole_faces = slots * lax.axis_size("tile") == 12
    if whole_faces and DEPTH * side == 128 and chans % 8 == 0 and K * chans <= 128:
        return face_path(features, out_grad, filters, tile_map)
    return general_path(features, out_grad, filters, tile_map)


def solution(mesh):
    placed = (P(("grp", "tile"), "sub", None), P(("grp", "tile"), "sub", None), P(), P())
    return jax.shard_map(
        on_device,
        mesh=mesh,
        in_specs=placed,
        out_specs=(P(("grp", "tile"), "sub", None), P("grp", "sub", None)),
        check_vma=False,
    )
```

```python
import functools
import math

import jax
import jax.numpy as jnp
import numpy as np
from jax import lax
from jax.experimental import pallas as pl
from jax.experimental.pallas import tpu as pltpu
from jax.sharding import PartitionSpec as P

K = 5


def from_behind(value, axis, steps):
    count = lax.axis_size(axis)
    pairs = [(source, (source + steps) % count) for source in range(count)]
    return lax.ppermute(value, axis, pairs)


def tile_coords(nested_code, bit_count):
    coord_x = nested_code * 0
    coord_y = nested_code * 0
    for bit_level in range(bit_count):
        coord_x = coord_x + nested_code // 4**bit_level % 2 * 2**bit_level
        coord_y = coord_y + nested_code // (2 * 4**bit_level) % 2 * 2**bit_level
    return (coord_x, coord_y)


def nested_index(coord_x, coord_y, bit_count):
    nested_code = coord_x * 0
    for bit_level in range(bit_count):
        nested_code = nested_code + coord_x // 2**bit_level % 2 * 4**bit_level
        nested_code = nested_code + coord_y // 2**bit_level % 2 * (2 * 4**bit_level)
    return nested_code


def pick(condition, when_true, when_false):
    return when_false + (when_true - when_false) * condition


def neighbour_codes(tile_ids, per_face, side_count):
    bit_count = side_count.bit_length() - 1
    face_id = tile_ids // per_face
    coord_x, coord_y = tile_coords(tile_ids % per_face, bit_count)
    column = face_id % 4
    is_north = face_id < 4
    is_south = face_id >= 8
    last_tile = side_count - 1

    def by_cycle(north_value, equator_value, south_value):
        return pick(is_north, north_value, pick(is_south, south_value, equator_value))

    side_rules = [
        (
            coord_x > 0,
            (face_id, coord_x - 1, coord_y, 1),
            (
                by_cycle(4 + column, 8 + (column + 3) % 4, 8 + (column + 3) % 4),
                by_cycle(last_tile, last_tile, coord_y),
                by_cycle(coord_y, coord_y, 0),
                by_cycle(1, 1, 2),
            ),
        ),
        (
            coord_x < last_tile,
            (face_id, coord_x + 1, coord_y, 0),
            (
                by_cycle((column + 1) % 4, column, 4 + (column + 1) % 4),
                by_cycle(coord_y, 0, 0),
                by_cycle(last_tile, coord_y, coord_y),
                by_cycle(3, 0, 0),
            ),
        ),
        (
            coord_y > 0,
            (face_id, coord_x, coord_y - 1, 3),
            (
                by_cycle(4 + (column + 1) % 4, 8 + column, 8 + (column + 1) % 4),
                by_cycle(coord_x, coord_x, 0),
                by_cycle(last_tile, last_tile, coord_x),
                by_cycle(3, 3, 0),
            ),
        ),
        (
            coord_y < last_tile,
            (face_id, coord_x, coord_y + 1, 2),
            (
                by_cycle((column + 3) % 4, (column + 3) % 4, 4 + column),
                by_cycle(last_tile, coord_x, coord_x),
                by_cycle(coord_x, 0, 0),
                by_cycle(1, 2, 2),
            ),
        ),
    ]
    target_list = []
    edge_list = []
    for inside, within, across in side_rules:
        chosen = [
            pick(inside, near_value, far_value) for near_value, far_value in zip(within, across)
        ]
        target_list.append(chosen[0] * per_face + nested_index(chosen[1], chosen[2], bit_count))
        edge_list.append(chosen[3] + tile_ids * 0)
    return (target_list, edge_list)


def neighbour_table(tile_map, per_face, side_count):
    target_list, edge_list = neighbour_codes(tile_map, per_face, side_count)
    targets = jnp.stack(target_list, axis=1).astype(jnp.int32)
    edges = jnp.stack(edge_list, axis=1).astype(jnp.int32)
    slot_of = jnp.argsort(tile_map).astype(jnp.int32)
    return (slot_of[targets].astype(jnp.int32), edges)


def peer_offsets(slot_count, device_count, per_face, side_count):
    tile_ids = np.arange(slot_count * device_count, dtype=np.int64)
    target_list, edge_list = neighbour_codes(tile_ids, per_face, side_count)
    targets = np.stack(target_list, axis=1)
    offsets = (tile_ids[:, None] // slot_count - targets // slot_count) % device_count
    distinct = sorted(set((int(value) for value in offsets.ravel())) - {0})
    position = np.zeros(device_count, dtype=np.int32)
    for order, value in enumerate(distinct):
        position[value] = order + 1
    return (distinct, position)


def edge_lines(values, tile_side):
    return jnp.stack(
        [
            values[..., :tile_side],
            values[..., -tile_side:],
            values[..., ::tile_side],
            values[..., tile_side - 1 :: tile_side],
        ],
        axis=1,
    )


def stencil(values, ghosts, tile_side):
    position = jnp.arange(values.shape[-1]) % tile_side
    zero_line = jnp.zeros_like(values[..., :1])
    upper_side = jnp.concatenate([ghosts[:, 0], values[..., :-tile_side]], axis=-1)
    lower_side = jnp.concatenate([values[..., tile_side:], ghosts[:, 1]], axis=-1)
    left_side = jnp.where(
        position == 0,
        jnp.repeat(ghosts[:, 2], tile_side, axis=-1),
        jnp.concatenate([zero_line, values[..., :-1]], axis=-1),
    )
    right_side = jnp.where(
        position == tile_side - 1,
        jnp.repeat(ghosts[:, 3], tile_side, axis=-1),
        jnp.concatenate([values[..., 1:], zero_line], axis=-1),
    )
    return -0.25 * (upper_side + lower_side + left_side + right_side)


def tile_total(filter_part):
    return lax.psum(filter_part, "tile")


def general_path(features, out_grad, filters, tile_map):
    slot_count = features.shape[0]
    group_channels = features.shape[1]
    tile_side = math.isqrt(features.shape[2])
    device_count = lax.axis_size("tile")
    total_tiles = slot_count * device_count
    side_count = math.isqrt(total_tiles // 12)
    scale_factor = 1.0 / math.sqrt(total_tiles * features.shape[2])
    highest = lax.Precision.HIGHEST
    slot_table, edge_table = neighbour_table(tile_map, total_tiles // 12, side_count)
    my_device = lax.axis_index("tile")
    first_slot = my_device * slot_count
    my_slots = lax.dynamic_slice_in_dim(slot_table, first_slot, slot_count, 0)
    my_edges = lax.dynamic_slice_in_dim(edge_table, first_slot, slot_count, 0)
    channel_start = lax.axis_index("sub") * group_channels
    weights = filters.astype(jnp.float32)
    distinct, position = peer_offsets(slot_count, device_count, total_tiles // 12, side_count)
    sender_gap = (my_device - my_slots // slot_count) % device_count
    local_rows = jnp.asarray(position)[sender_gap] * slot_count + my_slots % slot_count

    def laplace(values):
        border = edge_lines(values, tile_side).reshape(slot_count, 4, group_channels * tile_side)
        received = [border]
        for offset_value in distinct:
            received.append(from_behind(border, "tile", offset_value))
        stacked = jnp.concatenate(received, axis=0)
        stacked = stacked.reshape(stacked.shape[0], 4, group_channels, tile_side)
        ghosts = stacked[local_rows, my_edges]
        return stencil(values, ghosts, tile_side)

    whole_grad = lax.all_gather(out_grad, "sub", axis=1, tiled=True)
    cotangent = whole_grad.astype(jnp.float32)
    inputs = features.astype(jnp.float32)
    previous, current = (inputs, laplace(inputs))
    filter_terms = [
        jnp.einsum("sip,sop->io", inputs, cotangent, precision=highest),
        jnp.einsum("sip,sop->io", current, cotangent, precision=highest),
    ]
    for degree in range(2, K):
        previous, current = (current, 2.0 * laplace(current) - previous)
        filter_terms.append(jnp.einsum("sip,sop->io", current, cotangent, precision=highest))
    weight_grad = tile_total(jnp.stack(filter_terms)) * scale_factor
    row_block = lax.dynamic_slice_in_dim(weights, channel_start, group_channels, 1)

    def mixed(degree):
        return jnp.einsum("sop,io->sip", cotangent, row_block[degree], precision=highest)

    next_sum = mixed(K - 1)
    after_next = jnp.zeros_like(next_sum)
    for degree in range(K - 2, 0, -1):
        next_sum, after_next = (mixed(degree) + 2.0 * laplace(next_sum) - after_next, next_sum)
    in_grad = (mixed(0) + laplace(next_sum) - after_next).astype(jnp.bfloat16)
    return (in_grad, weight_grad)


DEPTH = K - 1
GHOST_SIDES = (0, 2, 3, 1)


def face_graph(tile_side):
    tile_ids = np.arange(12, dtype=np.int64)
    target_list, edge_list = neighbour_codes(tile_ids, 1, 1)
    targets = np.stack(target_list, axis=1)
    edges = np.stack(edge_list, axis=1)
    pixels = tile_side * tile_side
    grid = np.arange(pixels).reshape(tile_side, tile_side)
    lines = [grid[0], grid[-1], grid[:, 0], grid[:, -1]]
    ghosts = np.zeros((12, 4, tile_side), dtype=np.int64)
    around = np.zeros((12, 4, tile_side, tile_side), dtype=np.int64)
    for tile in range(12):
        for side in range(4):
            ghosts[tile, side] = targets[tile, side] * pixels + lines[edges[tile, side]]
        whole = tile * pixels + grid
        around[tile, 0] = np.concatenate([ghosts[tile, 0][None], whole[:-1]], 0)
        around[tile, 1] = np.concatenate([whole[1:], ghosts[tile, 1][None]], 0)
        around[tile, 2] = np.concatenate([ghosts[tile, 2][:, None], whole[:, :-1]], 1)
        around[tile, 3] = np.concatenate([whole[:, 1:], ghosts[tile, 3][:, None]], 1)
    around = around.transpose(0, 2, 3, 1).reshape(12 * pixels, 4)
    return targets, edges, ghosts, around


@functools.lru_cache(None)
def ghost_tables(tile_side):
    targets, edges, ghosts, around = face_graph(tile_side)
    pixels = tile_side * tile_side
    grid = np.arange(pixels).reshape(tile_side, tile_side)
    strips = np.stack(
        [
            grid[:DEPTH].ravel(),
            grid[-DEPTH:].ravel(),
            grid[:, :DEPTH].T.ravel(),
            grid[:, -DEPTH:].T.ravel(),
        ]
    )
    table = np.zeros((12, 10), dtype=np.int32)
    by_class = []
    for tile in range(12):
        wanted = np.concatenate([ghosts[tile, side] for side in GHOST_SIDES])
        power = np.zeros((wanted.size, 12 * pixels), dtype=np.int32)
        power[np.arange(wanted.size), wanted] = 1
        powers = [power]
        for _ in range(DEPTH - 1):
            powers.append(sum(powers[-1][:, around[:, side]] for side in range(4)))
        rows = np.concatenate(
            [powers[0], powers[1], powers[2] - 8 * powers[0], powers[3] - 12 * powers[1]]
        )
        support = np.flatnonzero(np.any(rows != 0, axis=0))
        sources = [(int(targets[tile, side]), int(edges[tile, side])) for side in range(4)]
        sources += [(tile, side) for side in range(4)]
        covered = set(int(t) * pixels + int(p) for t, e in sources for p in strips[e])
        left = [int(p) for p in support if int(p) not in covered]
        corner_tiles = {}
        for pixel in left:
            corner_tiles.setdefault(pixel // pixels, []).append(pixel % pixels)
        first = lambda t: int(
            np.flatnonzero(np.any(rows[:, [t * pixels + p for p in corner_tiles[t]]] != 0, axis=1))[0]
        )
        for other in sorted(corner_tiles, key=first):
            choice = [e for e in range(4) if set(corner_tiles[other]) <= set(strips[e].tolist())]
            sources.append((other, choice[0]))
        assert len(sources) <= 10
        while len(sources) < 10:
            sources.append(sources[-1])
        table[tile] = [t * 4 + e for t, e in sources]
        lanes = np.concatenate([t * pixels + strips[e] for t, e in sources])
        seen, keep = set(), np.zeros(lanes.size, dtype=bool)
        for lane, pixel in enumerate(lanes.tolist()):
            keep[lane] = pixel not in seen
            seen.add(pixel)
        assert set(support.tolist()) <= seen
        matrix = (rows[:, lanes] * keep[None]).T
        assert np.abs(matrix).max() <= 127
        if tile % 4 == 0:
            by_class.append(matrix)
        else:
            assert np.array_equal(matrix, by_class[-1])
    spread = np.zeros((4, tile_side, tile_side, tile_side), dtype=np.float32)
    step = np.arange(tile_side)
    spread[0, step, 0, step] = 1
    spread[1, step, step, 0] = 1
    spread[2, step, step, -1] = 1
    spread[3, step, -1, step] = 1
    spread = spread.reshape(4 * tile_side, pixels)
    take = np.zeros((pixels, 2 * DEPTH * tile_side), dtype=np.float32)
    take[np.concatenate([strips[2], strips[3]]), np.arange(2 * DEPTH * tile_side)] = 1
    return np.stack(by_class).astype(np.int8), table.reshape(-1), spread, take


def face_kernel(
    sizes,
    x_hbm,
    g_hbm,
    f_hbm,
    map_hbm,
    table_hbm,
    ghost_hbm,
    spread_hbm,
    take_hbm,
    in_ref,
    w_ref,
    strips,
    x_all,
    part,
    part_in,
    block,
    block_in,
    ghost_raw,
    ghost,
    spread,
    take,
    g_ref,
    f_ref,
    map_ref,
    table_ref,
    load_sem,
    s_send,
    s_recv,
    x_send,
    x_recv,
    p_send,
    p_recv,
    w_send,
    w_recv,
):
    slots, tiles_n, subs, side, scale = sizes
    chans = g_ref.shape[1]
    pixels = side * side
    width = DEPTH * side
    j = lax.axis_index("tile")
    s = lax.axis_index("sub")
    tile_peers = []
    for d in range(tiles_n - 1):
        up = d + (j <= d).astype(jnp.int32)
        back = tiles_n - 2 - d
        down = back + (j <= back).astype(jnp.int32)
        tile_peers.append(jnp.where(2 * j < tiles_n, down, up))
    sub_peers = [lax.rem(s + d, subs) for d in range(1, subs)]
    every = [(d, e) for d in range(tiles_n) for e in range(subs) if d + e > 0]

    def device(d, e):
        return {"tile": lax.rem(j + d, tiles_n), "sub": lax.rem(s + e, subs)}

    slot_loads = [
        pltpu.make_async_copy(map_hbm, map_ref, load_sem.at[0]),
        pltpu.make_async_copy(g_hbm, g_ref, load_sem.at[1]),
        pltpu.make_async_copy(take_hbm, take, load_sem.at[2]),
    ]
    for copy in slot_loads:
        copy.start()
    barrier = pltpu.get_barrier_semaphore()
    for d, e in every:
        pl.semaphore_signal(
            barrier, inc=1, device_id=device(d, e), device_id_type=pl.DeviceIdType.MESH
        )
    loads = [
        pltpu.make_async_copy(f_hbm, f_ref, load_sem.at[3]),
        pltpu.make_async_copy(table_hbm, table_ref, load_sem.at[4]),
        pltpu.make_async_copy(spread_hbm, spread, load_sem.at[5]),
        pltpu.make_async_copy(x_hbm, x_all.at[s], load_sem.at[6]),
    ]
    for m in range(slots):
        kind = (slots * j + m) // 4
        loads.append(
            pltpu.make_async_copy(ghost_hbm.at[kind], ghost_raw.at[m], load_sem.at[7 + m])
        )
    for copy in loads:
        copy.start()

    base = slots * j
    for copy in slot_loads:
        copy.wait()

    def slot_of(m):
        found = 0
        for slot in range(1, slots):
            found = jnp.where(map_ref[base + slot] == base + m, slot, found)
        return found

    slot_list = [slot_of(m) for m in range(slots)]
    own = [g_ref[slot_list[m]].astype(jnp.float32) for m in range(slots)]
    stacked = jnp.concatenate(own, axis=0).astype(jnp.bfloat16)
    cut = jnp.dot(stacked, take[...], preferred_element_type=jnp.float32)
    for m in range(slots):
        rows = slice(m * chans, (m + 1) * chans)
        row = (base + m) * 4
        strips[row] = own[m][:, :width].astype(jnp.bfloat16)
        strips[row + 1] = own[m][:, pixels - width :].astype(jnp.bfloat16)
        strips[row + 2] = cut[rows, :width].astype(jnp.bfloat16)
        strips[row + 3] = cut[rows, width:].astype(jnp.bfloat16)
    pl.semaphore_wait(barrier, len(every))

    def strip_copy(d, sender, target):
        mine = strips.at[pl.ds(sender * slots * 4, slots * 4)]
        return pltpu.make_async_remote_copy(
            mine,
            mine,
            s_send.at[d],
            s_recv.at[sender],
            device_id={"tile": target},
            device_id_type=pl.DeviceIdType.MESH,
        )

    def x_copy(d, sender, target):
        return pltpu.make_async_remote_copy(
            x_hbm,
            x_all.at[sender],
            x_send.at[d],
            x_recv.at[sender],
            device_id={"sub": target},
            device_id_type=pl.DeviceIdType.MESH,
        )

    def part_copy(m, d, sender, target):
        return pltpu.make_async_remote_copy(
            part.at[m, target],
            part_in.at[m, sender],
            p_send.at[m, d],
            p_recv.at[m, sender],
            device_id={"sub": target},
            device_id_type=pl.DeviceIdType.MESH,
        )

    def block_copy(order, d, e, sender):
        return pltpu.make_async_remote_copy(
            block.at[lax.rem(s + e, subs)],
            block_in.at[sender],
            w_send.at[order],
            w_recv.at[sender],
            device_id=device(d, e),
            device_id_type=pl.DeviceIdType.MESH,
        )

    for d, peer in enumerate(tile_peers):
        strip_copy(d, j, peer).start()
    for d, peer in enumerate(sub_peers):
        x_copy(d, s, peer).start()

    loads[0].wait()
    def mix(m):
        mixed = jnp.dot(mixing, terms[m], preferred_element_type=jnp.float32)
        for e in range(subs):
            part[m, e] = mixed[e * chans : (e + 1) * chans]
        for d, peer in enumerate(sub_peers):
            part_copy(m, d, s, peer).start()

    total_rows = (2 * K - 1) * chans
    row_k = lax.broadcasted_iota(jnp.int32, (subs * chans, total_rows), 1) // chans
    row_o = lax.broadcasted_iota(jnp.int32, (subs * chans, total_rows), 1) % chans
    from_o = lax.broadcasted_iota(jnp.int32, (subs * chans, total_rows), 0)
    mine_o = from_o == row_o + chans * s
    mixing = jnp.zeros((subs * chans, total_rows), jnp.float32)
    for k in range(K):
        chosen = jnp.where(mine_o & ((row_k + 1) // 2 == k), 1.0, 0.0).astype(jnp.bfloat16)
        mixing = mixing + jnp.dot(f_ref[k], chosen, preferred_element_type=jnp.float32)
    mixing = mixing.astype(jnp.bfloat16)

    for copy in loads[1:]:
        copy.wait()
    chunk = 128

    def widen(step, carry):
        at = pl.ds(pl.multiple_of(step * chunk, chunk), chunk)
        for m in range(slots):
            ghost[m, at, :] = ghost_raw[m, at, :].astype(jnp.float32).astype(jnp.bfloat16)
        return carry

    lax.fori_loop(0, ghost.shape[1] // chunk, widen, 0)

    for d, peer in enumerate(tile_peers):
        strip_copy(d, peer, peer).wait_recv()
    lane = lax.broadcasted_iota(jnp.int32, (chans, pixels), 1)
    y_at = lane % side
    scales = (1.0, -0.25, 0.125, -0.0625)
    grad = jnp.zeros((subs * chans, total_rows), jnp.float32)
    terms = []
    for m in range(slots):
        pieces = [
            strips[table_ref[(base + m) * 10 + r]].astype(jnp.float32) for r in range(10)
        ]
        source = jnp.concatenate(pieces, axis=1).astype(jnp.bfloat16)
        lines = jnp.dot(source, ghost[m], preferred_element_type=jnp.float32)
        lines = jnp.concatenate(
            [lines[:, k * 4 * side : (k + 1) * 4 * side] * scales[k] for k in range(DEPTH)], axis=0
        )
        high = lines.astype(jnp.bfloat16).astype(jnp.float32)
        rest = lines - high
        middle = rest.astype(jnp.bfloat16).astype(jnp.float32)
        split = jnp.concatenate([high, middle, rest - middle], axis=0).astype(jnp.bfloat16)
        outer = jnp.dot(split, spread[...], preferred_element_type=jnp.float32)
        count = DEPTH * chans
        outer = outer[:count] + outer[count : 2 * count] + outer[2 * count :]

        def around(value, k):
            total = outer[k * chans : (k + 1) * chans]
            total = total + jnp.where(lane < side, 0.0, pltpu.roll(value, side, 1))
            total = total + jnp.where(
                lane >= pixels - side, 0.0, pltpu.roll(value, pixels - side, 1)
            )
            total = total + jnp.where(y_at == 0, 0.0, pltpu.roll(value, 1, 1))
            return total + jnp.where(y_at == side - 1, 0.0, pltpu.roll(value, pixels - 1, 1))

        previous, current = own[m], -0.25 * around(own[m], 0)
        held = [previous]
        for k in range(1, K):
            high = current.astype(jnp.bfloat16).astype(jnp.float32)
            held += [high, current - high]
            if k < K - 1:
                previous, current = current, -0.5 * around(current, k) - previous
        term = jnp.concatenate(held, axis=0).astype(jnp.bfloat16)
        terms.append(term)
        if m < slots - 1:
            mix(m)

    for d, peer in enumerate(sub_peers):
        x_copy(d, peer, peer).wait_recv()
    for m in range(slots):
        maps = jnp.concatenate(
            [x_all[e, slot_list[m]].astype(jnp.float32) for e in range(subs)], axis=0
        ).astype(jnp.bfloat16)
        grad = grad + lax.dot_general(
            maps, terms[m], (((1,), (1,)), ((), ())), preferred_element_type=jnp.float32
        )
    sums = [grad[:, :chans]]
    for k in range(1, K):
        at = (2 * k - 1) * chans
        sums.append(grad[:, at : at + chans] + grad[:, at + chans : at + 2 * chans])
    sums.append(jnp.zeros((subs * chans, block.shape[2] - K * chans), jnp.float32))
    blocks = jnp.concatenate(sums, axis=1) * scale
    for e in range(subs):
        block[e] = blocks[e * chans : (e + 1) * chans]
    me = j * subs + s
    for order, (d, e) in enumerate(every):
        block_copy(order, d, e, me).start()
    mix(slots - 1)
    block_in[me] = block[s]

    for m in range(slots):
        for d, peer in enumerate(sub_peers):
            part_copy(m, d, peer, peer).wait_recv()
        part_in[m, s] = part[m, s]
    for slot in range(slots):
        m = lax.rem(map_ref[base + slot], slots)
        total = part_in[m, 0]
        for e in range(1, subs):
            total = total + part_in[m, e]
        in_ref[slot] = total.astype(in_ref.dtype)

    for order, (d, e) in enumerate(every):
        sender = lax.rem(j + d, tiles_n) * subs + lax.rem(s + e, subs)
        block_copy(order, d, e, sender).wait_recv()
    whole = []
    for e in range(subs):
        total = block_in[e]
        for t in range(1, tiles_n):
            total = total + block_in[t * subs + e]
        whole.append(total)
    for k in range(K):
        w_ref[k] = jnp.concatenate([v[:, k * chans : (k + 1) * chans] for v in whole], axis=1)

    for d, peer in enumerate(tile_peers):
        strip_copy(d, j, peer).wait_send()
    for d, peer in enumerate(sub_peers):
        x_copy(d, s, peer).wait_send()
        for m in range(slots):
            part_copy(m, d, s, peer).wait_send()
    for order, (d, e) in enumerate(every):
        block_copy(order, d, e, me).wait_send()


def face_path(features, out_grad, filters, tile_map):
    slots, chans, pixels = features.shape
    side = math.isqrt(pixels)
    tiles_n, subs = lax.axis_size("tile"), lax.axis_size("sub")
    matrices, table, spread, take = ghost_tables(side)
    scale = 1.0 / math.sqrt(slots * tiles_n * pixels)
    width = DEPTH * side
    vmem = pl.BlockSpec(memory_space=pltpu.VMEM)
    hbm = pl.BlockSpec(memory_space=pltpu.HBM)
    dma = pltpu.SemaphoreType.DMA
    return pl.pallas_call(
        functools.partial(face_kernel, (slots, tiles_n, subs, side, scale)),
        out_shape=(
            pltpu.VMEM(features.shape, jnp.bfloat16),
            pltpu.VMEM((K, chans, filters.shape[2]), jnp.float32),
        ),
        in_specs=[hbm] * 8,
        out_specs=(vmem, vmem),
        scratch_shapes=[
            pltpu.VMEM((slots * tiles_n * 4, chans, width), jnp.bfloat16),
            pltpu.VMEM((subs,) + features.shape, jnp.bfloat16),
            pltpu.VMEM((slots, subs, chans, pixels), jnp.float32),
            pltpu.VMEM((slots, subs, chans, pixels), jnp.float32),
            pltpu.VMEM((subs, chans, 128), jnp.float32),
            pltpu.VMEM((subs * tiles_n, chans, 128), jnp.float32),
            pltpu.VMEM((slots,) + matrices.shape[1:], jnp.int8),
            pltpu.VMEM((slots,) + matrices.shape[1:], jnp.bfloat16),
            pltpu.VMEM(spread.shape, jnp.bfloat16),
            pltpu.VMEM(take.shape, jnp.bfloat16),
            pltpu.VMEM(features.shape, jnp.bfloat16),
            pltpu.VMEM(filters.shape, jnp.bfloat16),
            pltpu.SMEM(tile_map.shape, jnp.int32),
            pltpu.SMEM(table.shape, jnp.int32),
            dma((7 + slots,)),
            dma((tiles_n,)),
            dma((tiles_n,)),
            dma((subs,)),
            dma((subs,)),
            dma((slots, subs)),
            dma((slots, subs)),
            dma((subs * tiles_n,)),
            dma((subs * tiles_n,)),
        ],
        compiler_params=pltpu.CompilerParams(
            collective_id=0, has_side_effects=True, vmem_limit_bytes=67043328 - 512 * 1024
        ),
    )(
        features,
        out_grad,
        filters,
        tile_map,
        jnp.asarray(table),
        jnp.asarray(matrices),
        jnp.asarray(spread, jnp.bfloat16),
        jnp.asarray(take, jnp.bfloat16),
    )


def on_device(features, out_grad, filters, tile_map):
    slots, chans, pixels = features.shape
    side = math.isqrt(pixels)
    whole_faces = slots * lax.axis_size("tile") == 12
    if whole_faces and DEPTH * side == 128 and chans % 8 == 0 and K * chans <= 128:
        return face_path(features, out_grad, filters, tile_map)
    return general_path(features, out_grad, filters, tile_map)


def solution(mesh):
    placed = (P(("grp", "tile"), "sub", None), P(("grp", "tile"), "sub", None), P(), P())
    return jax.shard_map(
        on_device,
        mesh=mesh,
        in_specs=placed,
        out_specs=(P(("grp", "tile"), "sub", None), P("grp", "sub", None)),
        check_vma=False,
    )
```

```python
import functools
import math

import jax
import jax.numpy as jnp
import numpy as np
from jax import lax
from jax.experimental import pallas as pl
from jax.experimental.pallas import tpu as pltpu
from jax.sharding import PartitionSpec as P

K = 5


def from_behind(value, axis, steps):
    count = lax.axis_size(axis)
    pairs = [(source, (source + steps) % count) for source in range(count)]
    return lax.ppermute(value, axis, pairs)


def tile_coords(nested_code, bit_count):
    coord_x = nested_code * 0
    coord_y = nested_code * 0
    for bit_level in range(bit_count):
        coord_x = coord_x + nested_code // 4**bit_level % 2 * 2**bit_level
        coord_y = coord_y + nested_code // (2 * 4**bit_level) % 2 * 2**bit_level
    return (coord_x, coord_y)


def nested_index(coord_x, coord_y, bit_count):
    nested_code = coord_x * 0
    for bit_level in range(bit_count):
        nested_code = nested_code + coord_x // 2**bit_level % 2 * 4**bit_level
        nested_code = nested_code + coord_y // 2**bit_level % 2 * (2 * 4**bit_level)
    return nested_code


def pick(condition, when_true, when_false):
    return when_false + (when_true - when_false) * condition


def neighbour_codes(tile_ids, per_face, side_count):
    bit_count = side_count.bit_length() - 1
    face_id = tile_ids // per_face
    coord_x, coord_y = tile_coords(tile_ids % per_face, bit_count)
    column = face_id % 4
    is_north = face_id < 4
    is_south = face_id >= 8
    last_tile = side_count - 1

    def by_cycle(north_value, equator_value, south_value):
        return pick(is_north, north_value, pick(is_south, south_value, equator_value))

    side_rules = [
        (
            coord_x > 0,
            (face_id, coord_x - 1, coord_y, 1),
            (
                by_cycle(4 + column, 8 + (column + 3) % 4, 8 + (column + 3) % 4),
                by_cycle(last_tile, last_tile, coord_y),
                by_cycle(coord_y, coord_y, 0),
                by_cycle(1, 1, 2),
            ),
        ),
        (
            coord_x < last_tile,
            (face_id, coord_x + 1, coord_y, 0),
            (
                by_cycle((column + 1) % 4, column, 4 + (column + 1) % 4),
                by_cycle(coord_y, 0, 0),
                by_cycle(last_tile, coord_y, coord_y),
                by_cycle(3, 0, 0),
            ),
        ),
        (
            coord_y > 0,
            (face_id, coord_x, coord_y - 1, 3),
            (
                by_cycle(4 + (column + 1) % 4, 8 + column, 8 + (column + 1) % 4),
                by_cycle(coord_x, coord_x, 0),
                by_cycle(last_tile, last_tile, coord_x),
                by_cycle(3, 3, 0),
            ),
        ),
        (
            coord_y < last_tile,
            (face_id, coord_x, coord_y + 1, 2),
            (
                by_cycle((column + 3) % 4, (column + 3) % 4, 4 + column),
                by_cycle(last_tile, coord_x, coord_x),
                by_cycle(coord_x, 0, 0),
                by_cycle(1, 2, 2),
            ),
        ),
    ]
    target_list = []
    edge_list = []
    for inside, within, across in side_rules:
        chosen = [
            pick(inside, near_value, far_value) for near_value, far_value in zip(within, across)
        ]
        target_list.append(chosen[0] * per_face + nested_index(chosen[1], chosen[2], bit_count))
        edge_list.append(chosen[3] + tile_ids * 0)
    return (target_list, edge_list)


def neighbour_table(tile_map, per_face, side_count):
    target_list, edge_list = neighbour_codes(tile_map, per_face, side_count)
    targets = jnp.stack(target_list, axis=1).astype(jnp.int32)
    edges = jnp.stack(edge_list, axis=1).astype(jnp.int32)
    slot_of = jnp.argsort(tile_map).astype(jnp.int32)
    return (slot_of[targets].astype(jnp.int32), edges)


def peer_offsets(slot_count, device_count, per_face, side_count):
    tile_ids = np.arange(slot_count * device_count, dtype=np.int64)
    target_list, edge_list = neighbour_codes(tile_ids, per_face, side_count)
    targets = np.stack(target_list, axis=1)
    offsets = (tile_ids[:, None] // slot_count - targets // slot_count) % device_count
    distinct = sorted(set((int(value) for value in offsets.ravel())) - {0})
    position = np.zeros(device_count, dtype=np.int32)
    for order, value in enumerate(distinct):
        position[value] = order + 1
    return (distinct, position)


def edge_lines(values, tile_side):
    return jnp.stack(
        [
            values[..., :tile_side],
            values[..., -tile_side:],
            values[..., ::tile_side],
            values[..., tile_side - 1 :: tile_side],
        ],
        axis=1,
    )


def stencil(values, ghosts, tile_side):
    position = jnp.arange(values.shape[-1]) % tile_side
    zero_line = jnp.zeros_like(values[..., :1])
    upper_side = jnp.concatenate([ghosts[:, 0], values[..., :-tile_side]], axis=-1)
    lower_side = jnp.concatenate([values[..., tile_side:], ghosts[:, 1]], axis=-1)
    left_side = jnp.where(
        position == 0,
        jnp.repeat(ghosts[:, 2], tile_side, axis=-1),
        jnp.concatenate([zero_line, values[..., :-1]], axis=-1),
    )
    right_side = jnp.where(
        position == tile_side - 1,
        jnp.repeat(ghosts[:, 3], tile_side, axis=-1),
        jnp.concatenate([values[..., 1:], zero_line], axis=-1),
    )
    return -0.25 * (upper_side + lower_side + left_side + right_side)


def tile_total(filter_part):
    return lax.psum(filter_part, "tile")


def general_path(features, out_grad, filters, tile_map):
    slot_count = features.shape[0]
    group_channels = features.shape[1]
    tile_side = math.isqrt(features.shape[2])
    device_count = lax.axis_size("tile")
    total_tiles = slot_count * device_count
    side_count = math.isqrt(total_tiles // 12)
    scale_factor = 1.0 / math.sqrt(total_tiles * features.shape[2])
    highest = lax.Precision.HIGHEST
    slot_table, edge_table = neighbour_table(tile_map, total_tiles // 12, side_count)
    my_device = lax.axis_index("tile")
    first_slot = my_device * slot_count
    my_slots = lax.dynamic_slice_in_dim(slot_table, first_slot, slot_count, 0)
    my_edges = lax.dynamic_slice_in_dim(edge_table, first_slot, slot_count, 0)
    channel_start = lax.axis_index("sub") * group_channels
    weights = filters.astype(jnp.float32)
    distinct, position = peer_offsets(slot_count, device_count, total_tiles // 12, side_count)
    sender_gap = (my_device - my_slots // slot_count) % device_count
    local_rows = jnp.asarray(position)[sender_gap] * slot_count + my_slots % slot_count

    def laplace(values):
        border = edge_lines(values, tile_side).reshape(slot_count, 4, group_channels * tile_side)
        received = [border]
        for offset_value in distinct:
            received.append(from_behind(border, "tile", offset_value))
        stacked = jnp.concatenate(received, axis=0)
        stacked = stacked.reshape(stacked.shape[0], 4, group_channels, tile_side)
        ghosts = stacked[local_rows, my_edges]
        return stencil(values, ghosts, tile_side)

    whole_grad = lax.all_gather(out_grad, "sub", axis=1, tiled=True)
    cotangent = whole_grad.astype(jnp.float32)
    inputs = features.astype(jnp.float32)
    previous, current = (inputs, laplace(inputs))
    filter_terms = [
        jnp.einsum("sip,sop->io", inputs, cotangent, precision=highest),
        jnp.einsum("sip,sop->io", current, cotangent, precision=highest),
    ]
    for degree in range(2, K):
        previous, current = (current, 2.0 * laplace(current) - previous)
        filter_terms.append(jnp.einsum("sip,sop->io", current, cotangent, precision=highest))
    weight_grad = tile_total(jnp.stack(filter_terms)) * scale_factor
    row_block = lax.dynamic_slice_in_dim(weights, channel_start, group_channels, 1)

    def mixed(degree):
        return jnp.einsum("sop,io->sip", cotangent, row_block[degree], precision=highest)

    next_sum = mixed(K - 1)
    after_next = jnp.zeros_like(next_sum)
    for degree in range(K - 2, 0, -1):
        next_sum, after_next = (mixed(degree) + 2.0 * laplace(next_sum) - after_next, next_sum)
    in_grad = (mixed(0) + laplace(next_sum) - after_next).astype(jnp.bfloat16)
    return (in_grad, weight_grad)


DEPTH = K - 1
GHOST_SIDES = (0, 2, 3, 1)


def face_graph(tile_side):
    tile_ids = np.arange(12, dtype=np.int64)
    target_list, edge_list = neighbour_codes(tile_ids, 1, 1)
    targets = np.stack(target_list, axis=1)
    edges = np.stack(edge_list, axis=1)
    pixels = tile_side * tile_side
    grid = np.arange(pixels).reshape(tile_side, tile_side)
    lines = [grid[0], grid[-1], grid[:, 0], grid[:, -1]]
    ghosts = np.zeros((12, 4, tile_side), dtype=np.int64)
    around = np.zeros((12, 4, tile_side, tile_side), dtype=np.int64)
    for tile in range(12):
        for side in range(4):
            ghosts[tile, side] = targets[tile, side] * pixels + lines[edges[tile, side]]
        whole = tile * pixels + grid
        around[tile, 0] = np.concatenate([ghosts[tile, 0][None], whole[:-1]], 0)
        around[tile, 1] = np.concatenate([whole[1:], ghosts[tile, 1][None]], 0)
        around[tile, 2] = np.concatenate([ghosts[tile, 2][:, None], whole[:, :-1]], 1)
        around[tile, 3] = np.concatenate([whole[:, 1:], ghosts[tile, 3][:, None]], 1)
    around = around.transpose(0, 2, 3, 1).reshape(12 * pixels, 4)
    return targets, edges, ghosts, around


@functools.lru_cache(None)
def ghost_tables(tile_side):
    targets, edges, ghosts, around = face_graph(tile_side)
    pixels = tile_side * tile_side
    grid = np.arange(pixels).reshape(tile_side, tile_side)
    strips = np.stack(
        [
            grid[:DEPTH].ravel(),
            grid[-DEPTH:].ravel(),
            grid[:, :DEPTH].T.ravel(),
            grid[:, -DEPTH:].T.ravel(),
        ]
    )
    table = np.zeros((12, 10), dtype=np.int32)
    by_class = []
    for tile in range(12):
        wanted = np.concatenate([ghosts[tile, side] for side in GHOST_SIDES])
        power = np.zeros((wanted.size, 12 * pixels), dtype=np.int32)
        power[np.arange(wanted.size), wanted] = 1
        powers = [power]
        for _ in range(DEPTH - 1):
            powers.append(sum(powers[-1][:, around[:, side]] for side in range(4)))
        rows = np.concatenate(
            [powers[0], powers[1], powers[2] - 8 * powers[0], powers[3] - 12 * powers[1]]
        )
        support = np.flatnonzero(np.any(rows != 0, axis=0))
        sources = [(int(targets[tile, side]), int(edges[tile, side])) for side in range(4)]
        sources += [(tile, side) for side in range(4)]
        covered = set(int(t) * pixels + int(p) for t, e in sources for p in strips[e])
        left = [int(p) for p in support if int(p) not in covered]
        corner_tiles = {}
        for pixel in left:
            corner_tiles.setdefault(pixel // pixels, []).append(pixel % pixels)
        first = lambda t: int(
            np.flatnonzero(np.any(rows[:, [t * pixels + p for p in corner_tiles[t]]] != 0, axis=1))[0]
        )
        for other in sorted(corner_tiles, key=first):
            choice = [e for e in range(4) if set(corner_tiles[other]) <= set(strips[e].tolist())]
            sources.append((other, choice[0]))
        assert len(sources) <= 10
        while len(sources) < 10:
            sources.append(sources[-1])
        table[tile] = [t * 4 + e for t, e in sources]
        lanes = np.concatenate([t * pixels + strips[e] for t, e in sources])
        seen, keep = set(), np.zeros(lanes.size, dtype=bool)
        for lane, pixel in enumerate(lanes.tolist()):
            keep[lane] = pixel not in seen
            seen.add(pixel)
        assert set(support.tolist()) <= seen
        matrix = (rows[:, lanes] * keep[None]).T
        assert np.abs(matrix).max() <= 127
        if tile % 4 == 0:
            by_class.append(matrix)
        else:
            assert np.array_equal(matrix, by_class[-1])
    spread = np.zeros((4, tile_side, tile_side, tile_side), dtype=np.float32)
    step = np.arange(tile_side)
    spread[0, step, 0, step] = 1
    spread[1, step, step, 0] = 1
    spread[2, step, step, -1] = 1
    spread[3, step, -1, step] = 1
    spread = spread.reshape(4 * tile_side, pixels)
    take = np.zeros((pixels, 2 * DEPTH * tile_side), dtype=np.float32)
    take[np.concatenate([strips[2], strips[3]]), np.arange(2 * DEPTH * tile_side)] = 1
    return np.stack(by_class).astype(np.int8), table.reshape(-1), spread, take


def face_kernel(
    sizes,
    x_hbm,
    g_hbm,
    f_hbm,
    map_hbm,
    table_hbm,
    ghost_hbm,
    spread_hbm,
    take_hbm,
    in_ref,
    w_ref,
    strips,
    x_all,
    part,
    part_in,
    block,
    block_in,
    ghost_raw,
    ghost,
    spread,
    take,
    g_ref,
    f_ref,
    map_ref,
    table_ref,
    known,
    load_sem,
    s_send,
    s_recv,
    x_send,
    x_recv,
    p_send,
    p_recv,
    w_send,
    w_recv,
):
    slots, tiles_n, subs, side, scale = sizes
    chans = g_ref.shape[1]
    pixels = side * side
    width = DEPTH * side
    j = lax.axis_index("tile")
    s = lax.axis_index("sub")
    tile_peers = []
    for d in range(tiles_n - 1):
        up = d + (j <= d).astype(jnp.int32)
        back = tiles_n - 2 - d
        down = back + (j <= back).astype(jnp.int32)
        tile_peers.append(jnp.where(2 * j < tiles_n, down, up))
    sub_peers = [lax.rem(s + d, subs) for d in range(1, subs)]
    every = [(d, e) for d in range(tiles_n) for e in range(subs) if d + e > 0]

    def device(d, e):
        return {"tile": lax.rem(j + d, tiles_n), "sub": lax.rem(s + e, subs)}

    slot_loads = [
        pltpu.make_async_copy(map_hbm, map_ref, load_sem.at[0]),
        pltpu.make_async_copy(g_hbm, g_ref, load_sem.at[1]),
        pltpu.make_async_copy(take_hbm, take, load_sem.at[2]),
    ]
    for copy in slot_loads:
        copy.start()
    barrier = pltpu.get_barrier_semaphore()
    friends = [{"tile": peer} for peer in tile_peers] + [{"sub": peer} for peer in sub_peers]
    for friend in friends:
        pl.semaphore_signal(
            barrier, inc=1, device_id=friend, device_id_type=pl.DeviceIdType.MESH
        )
    loads = [
        pltpu.make_async_copy(f_hbm, f_ref, load_sem.at[3]),
        pltpu.make_async_copy(table_hbm, table_ref, load_sem.at[4]),
        pltpu.make_async_copy(spread_hbm, spread, load_sem.at[5]),
        pltpu.make_async_copy(x_hbm, x_all.at[s], load_sem.at[6]),
    ]
    for m in range(slots):
        kind = (slots * j + m) // 4
        loads.append(
            pltpu.make_async_copy(ghost_hbm.at[kind], ghost_raw.at[m], load_sem.at[7 + m])
        )
    for copy in loads:
        copy.start()

    base = slots * j
    for copy in slot_loads:
        copy.wait()

    def slot_of(m):
        found = 0
        for slot in range(1, slots):
            found = jnp.where(map_ref[base + slot] == base + m, slot, found)
        return found

    slot_list = [slot_of(m) for m in range(slots)]
    own = [g_ref[slot_list[m]].astype(jnp.float32) for m in range(slots)]
    stacked = jnp.concatenate(own, axis=0).astype(jnp.bfloat16)
    cut = jnp.dot(stacked, take[...], preferred_element_type=jnp.float32)
    for m in range(slots):
        rows = slice(m * chans, (m + 1) * chans)
        row = (base + m) * 4
        strips[row] = own[m][:, :width].astype(jnp.bfloat16)
        strips[row + 1] = own[m][:, pixels - width :].astype(jnp.bfloat16)
        strips[row + 2] = cut[rows, :width].astype(jnp.bfloat16)
        strips[row + 3] = cut[rows, width:].astype(jnp.bfloat16)
    pl.semaphore_wait(barrier, len(friends))
    for peer in sub_peers:
        pl.semaphore_signal(
            known, inc=1, device_id={"sub": peer}, device_id_type=pl.DeviceIdType.MESH
        )

    def strip_copy(d, sender, target):
        mine = strips.at[pl.ds(sender * slots * 4, slots * 4)]
        return pltpu.make_async_remote_copy(
            mine,
            mine,
            s_send.at[d],
            s_recv.at[sender],
            device_id={"tile": target},
            device_id_type=pl.DeviceIdType.MESH,
        )

    def x_copy(d, sender, target):
        return pltpu.make_async_remote_copy(
            x_hbm,
            x_all.at[sender],
            x_send.at[d],
            x_recv.at[sender],
            device_id={"sub": target},
            device_id_type=pl.DeviceIdType.MESH,
        )

    def part_copy(m, d, sender, target):
        return pltpu.make_async_remote_copy(
            part.at[m, target],
            part_in.at[m, sender],
            p_send.at[m, d],
            p_recv.at[m, sender],
            device_id={"sub": target},
            device_id_type=pl.DeviceIdType.MESH,
        )

    def block_copy(order, d, e, sender):
        return pltpu.make_async_remote_copy(
            block.at[lax.rem(s + e, subs)],
            block_in.at[sender],
            w_send.at[order],
            w_recv.at[sender],
            device_id=device(d, e),
            device_id_type=pl.DeviceIdType.MESH,
        )

    for d, peer in enumerate(tile_peers):
        strip_copy(d, j, peer).start()
    for d, peer in enumerate(sub_peers):
        x_copy(d, s, peer).start()

    loads[0].wait()
    def mix(m):
        mixed = jnp.dot(mixing, terms[m], preferred_element_type=jnp.float32)
        for e in range(subs):
            part[m, e] = mixed[e * chans : (e + 1) * chans]
        for d, peer in enumerate(sub_peers):
            part_copy(m, d, s, peer).start()

    total_rows = (2 * K - 1) * chans
    row_k = lax.broadcasted_iota(jnp.int32, (subs * chans, total_rows), 1) // chans
    row_o = lax.broadcasted_iota(jnp.int32, (subs * chans, total_rows), 1) % chans
    from_o = lax.broadcasted_iota(jnp.int32, (subs * chans, total_rows), 0)
    mine_o = from_o == row_o + chans * s
    mixing = jnp.zeros((subs * chans, total_rows), jnp.float32)
    for k in range(K):
        chosen = jnp.where(mine_o & ((row_k + 1) // 2 == k), 1.0, 0.0).astype(jnp.bfloat16)
        mixing = mixing + jnp.dot(f_ref[k], chosen, preferred_element_type=jnp.float32)
    mixing = mixing.astype(jnp.bfloat16)

    for copy in loads[1:]:
        copy.wait()
    chunk = 128

    def widen(step, carry):
        at = pl.ds(pl.multiple_of(step * chunk, chunk), chunk)
        for m in range(slots):
            ghost[m, at, :] = ghost_raw[m, at, :].astype(jnp.float32).astype(jnp.bfloat16)
        return carry

    lax.fori_loop(0, ghost.shape[1] // chunk, widen, 0)

    for d, peer in enumerate(tile_peers):
        strip_copy(d, peer, peer).wait_recv()
    lane = lax.broadcasted_iota(jnp.int32, (chans, pixels), 1)
    y_at = lane % side
    scales = (1.0, -0.25, 0.125, -0.0625)
    grad = jnp.zeros((subs * chans, total_rows), jnp.float32)
    terms = []
    for m in range(slots):
        pieces = [
            strips[table_ref[(base + m) * 10 + r]].astype(jnp.float32) for r in range(10)
        ]
        source = jnp.concatenate(pieces, axis=1).astype(jnp.bfloat16)
        lines = jnp.dot(source, ghost[m], preferred_element_type=jnp.float32)
        lines = jnp.concatenate(
            [lines[:, k * 4 * side : (k + 1) * 4 * side] * scales[k] for k in range(DEPTH)], axis=0
        )
        high = lines.astype(jnp.bfloat16).astype(jnp.float32)
        rest = lines - high
        middle = rest.astype(jnp.bfloat16).astype(jnp.float32)
        split = jnp.concatenate([high, middle, rest - middle], axis=0).astype(jnp.bfloat16)
        outer = jnp.dot(split, spread[...], preferred_element_type=jnp.float32)
        count = DEPTH * chans
        outer = outer[:count] + outer[count : 2 * count] + outer[2 * count :]

        def around(value, k):
            total = outer[k * chans : (k + 1) * chans]
            total = total + jnp.where(lane < side, 0.0, pltpu.roll(value, side, 1))
            total = total + jnp.where(
                lane >= pixels - side, 0.0, pltpu.roll(value, pixels - side, 1)
            )
            total = total + jnp.where(y_at == 0, 0.0, pltpu.roll(value, 1, 1))
            return total + jnp.where(y_at == side - 1, 0.0, pltpu.roll(value, pixels - 1, 1))

        previous, current = own[m], -0.25 * around(own[m], 0)
        held = [previous]
        for k in range(1, K):
            high = current.astype(jnp.bfloat16).astype(jnp.float32)
            held += [high, current - high]
            if k < K - 1:
                previous, current = current, -0.5 * around(current, k) - previous
        term = jnp.concatenate(held, axis=0).astype(jnp.bfloat16)
        terms.append(term)
        if m < slots - 1:
            mix(m)

    for d, peer in enumerate(sub_peers):
        x_copy(d, peer, peer).wait_recv()
    for m in range(slots):
        maps = jnp.concatenate(
            [x_all[e, slot_list[m]].astype(jnp.float32) for e in range(subs)], axis=0
        ).astype(jnp.bfloat16)
        grad = grad + lax.dot_general(
            maps, terms[m], (((1,), (1,)), ((), ())), preferred_element_type=jnp.float32
        )
    sums = [grad[:, :chans]]
    for k in range(1, K):
        at = (2 * k - 1) * chans
        sums.append(grad[:, at : at + chans] + grad[:, at + chans : at + 2 * chans])
    sums.append(jnp.zeros((subs * chans, block.shape[2] - K * chans), jnp.float32))
    blocks = jnp.concatenate(sums, axis=1) * scale
    for e in range(subs):
        block[e] = blocks[e * chans : (e + 1) * chans]
    me = j * subs + s
    pl.semaphore_wait(known, subs - 1)
    for order, (d, e) in enumerate(every):
        block_copy(order, d, e, me).start()
    mix(slots - 1)
    block_in[me] = block[s]

    for m in range(slots):
        for d, peer in enumerate(sub_peers):
            part_copy(m, d, peer, peer).wait_recv()
        part_in[m, s] = part[m, s]
    for slot in range(slots):
        m = lax.rem(map_ref[base + slot], slots)
        total = part_in[m, 0]
        for e in range(1, subs):
            total = total + part_in[m, e]
        in_ref[slot] = total.astype(in_ref.dtype)

    for order, (d, e) in enumerate(every):
        sender = lax.rem(j + d, tiles_n) * subs + lax.rem(s + e, subs)
        block_copy(order, d, e, sender).wait_recv()
    whole = []
    for e in range(subs):
        total = block_in[e]
        for t in range(1, tiles_n):
            total = total + block_in[t * subs + e]
        whole.append(total)
    for k in range(K):
        w_ref[k] = jnp.concatenate([v[:, k * chans : (k + 1) * chans] for v in whole], axis=1)

    for d, peer in enumerate(tile_peers):
        strip_copy(d, j, peer).wait_send()
    for d, peer in enumerate(sub_peers):
        x_copy(d, s, peer).wait_send()
        for m in range(slots):
            part_copy(m, d, s, peer).wait_send()
    for order, (d, e) in enumerate(every):
        block_copy(order, d, e, me).wait_send()


def face_path(features, out_grad, filters, tile_map):
    slots, chans, pixels = features.shape
    side = math.isqrt(pixels)
    tiles_n, subs = lax.axis_size("tile"), lax.axis_size("sub")
    matrices, table, spread, take = ghost_tables(side)
    scale = 1.0 / math.sqrt(slots * tiles_n * pixels)
    width = DEPTH * side
    vmem = pl.BlockSpec(memory_space=pltpu.VMEM)
    hbm = pl.BlockSpec(memory_space=pltpu.HBM)
    dma = pltpu.SemaphoreType.DMA
    return pl.pallas_call(
        functools.partial(face_kernel, (slots, tiles_n, subs, side, scale)),
        out_shape=(
            pltpu.VMEM(features.shape, jnp.bfloat16),
            pltpu.VMEM((K, chans, filters.shape[2]), jnp.float32),
        ),
        in_specs=[hbm] * 8,
        out_specs=(vmem, vmem),
        scratch_shapes=[
            pltpu.VMEM((slots * tiles_n * 4, chans, width), jnp.bfloat16),
            pltpu.VMEM((subs,) + features.shape, jnp.bfloat16),
            pltpu.VMEM((slots, subs, chans, pixels), jnp.float32),
            pltpu.VMEM((slots, subs, chans, pixels), jnp.float32),
            pltpu.VMEM((subs, chans, 128), jnp.float32),
            pltpu.VMEM((subs * tiles_n, chans, 128), jnp.float32),
            pltpu.VMEM((slots,) + matrices.shape[1:], jnp.int8),
            pltpu.VMEM((slots,) + matrices.shape[1:], jnp.bfloat16),
            pltpu.VMEM(spread.shape, jnp.bfloat16),
            pltpu.VMEM(take.shape, jnp.bfloat16),
            pltpu.VMEM(features.shape, jnp.bfloat16),
            pltpu.VMEM(filters.shape, jnp.bfloat16),
            pltpu.SMEM(tile_map.shape, jnp.int32),
            pltpu.SMEM(table.shape, jnp.int32),
            pltpu.SemaphoreType.REGULAR,
            dma((7 + slots,)),
            dma((tiles_n,)),
            dma((tiles_n,)),
            dma((subs,)),
            dma((subs,)),
            dma((slots, subs)),
            dma((slots, subs)),
            dma((subs * tiles_n,)),
            dma((subs * tiles_n,)),
        ],
        compiler_params=pltpu.CompilerParams(
            collective_id=0, has_side_effects=True, vmem_limit_bytes=67043328 - 512 * 1024
        ),
    )(
        features,
        out_grad,
        filters,
        tile_map,
        jnp.asarray(table),
        jnp.asarray(matrices),
        jnp.asarray(spread, jnp.bfloat16),
        jnp.asarray(take, jnp.bfloat16),
    )


def on_device(features, out_grad, filters, tile_map):
    slots, chans, pixels = features.shape
    side = math.isqrt(pixels)
    whole_faces = slots * lax.axis_size("tile") == 12
    if whole_faces and DEPTH * side == 128 and chans % 8 == 0 and K * chans <= 128:
        return face_path(features, out_grad, filters, tile_map)
    return general_path(features, out_grad, filters, tile_map)


def solution(mesh):
    placed = (P(("grp", "tile"), "sub", None), P(("grp", "tile"), "sub", None), P(), P())
    return jax.shard_map(
        on_device,
        mesh=mesh,
        in_specs=placed,
        out_specs=(P(("grp", "tile"), "sub", None), P("grp", "sub", None)),
        check_vma=False,
    )
```
